256 devices in a mesh: dp: 64 (over z_hi, y, x), tensor: 4 (over z_lo, core).
Axes of the slice: x: 4, y: 4, z: 8 (z_hi: 4, z_lo: 2; z = z_hi * 2 + z_lo), core: 2. Of those that a mesh axis runs over, the one named last changes fastest.
Arguments:
- hidden: bfloat16 [32768, 8192], P('dp', 'tensor'), may hold values from -16 to 16
- kv_weight: bfloat16 [8192, 1024], P(None, 'tensor'), may hold values from -0.0625 to 0.0625
- queries: bfloat16 [32768, 4096], P('dp', 'tensor'), may hold values from -28 to 28
- out_grad: bfloat16 [32768, 4096], P('dp', 'tensor'), may hold values from -6 to 6
- live_blocks: int32 [64], P('dp'), may hold values from 0 to 4, as said below
- doc_start: int32 [32768], P('dp'), may hold values from 0 to 127, as said below
Outputs:
- q_grad: bfloat16 [32768, 4096], P('dp', 'tensor')
- hidden_grad: bfloat16 [32768, 8192], P('dp', 'tensor')
- kv_weight_grad: float32 [8192, 1024], P('dp', 'tensor')
The draws below stay inside these ranges and needn't reach their ends.
Inputs may be any that keep to these rules, and one draw needn't show every extreme that they name: live_blocks[i] + live_blocks[j] = 4 for the two indices i and j of dp that lie half the axis apart; the live blocks of an index are its first ones. doc_start of a row is at most its own position within its block, position 0 of every block is 0, and the rows of one document are consecutive.
All inputs are finite; a program needn't handle non-finite values.
Results may differ from the reference program's by a relative error of at most 0.014.
The reference program's roundings to bfloat16 on the way count: a program that leaves them out, or rounds other values in their place, can miss the bound.
Values may be sent and summed in bfloat16 or wider, within the bound.
A program may use at most 128 MiB of HBM per device.

```python
import jax
import jax.numpy as jnp
from jax import lax

D = 8192
HEADS = 32
KV_HEADS = 4
HEAD_DIM = 128
BLOCK = 128
NBLK = 4
TOK_DEV = 512
TOKENS = 32768
N_DP = 64
N_TENSOR = 4


def draw_queries(key, part):
    values_out = jnp.clip(jax.random.normal(key, (TOKENS, HEADS, HEAD_DIM), jnp.float32), -4.0, 4.0)
    return values_out.reshape(TOKENS, HEADS * HEAD_DIM).astype(jnp.bfloat16)


def draw_doc_start(key, part):
    block_total = TOKENS // BLOCK
    starts_flag = jax.random.randint(key, (block_total, BLOCK), 0, max(2, BLOCK // 4)) == 0
    position = jnp.arange(BLOCK, dtype=jnp.int32)
    chosen_block = jax.random.randint(jax.random.fold_in(key, 3), (), 0, block_total)
    forced = (jnp.arange(block_total)[:, None] == chosen_block) & (position[None, :] == BLOCK - 1)
    marked = starts_flag | forced | (position[None, :] == 0)
    begins = jnp.where(marked, position[None, :], 0).astype(jnp.int32)
    return lax.cummax(begins, axis=1).reshape(TOKENS).astype(jnp.int32)


def draw_live_blocks(key, part):
    half_axis = TOKENS // TOK_DEV // 2
    first_half = jax.random.randint(key, (half_axis,), 0, NBLK + 1)
    chosen = jax.random.randint(jax.random.fold_in(key, 5), (), 0, half_axis)
    first_half = jnp.where(jnp.arange(half_axis) == chosen, NBLK, first_half)
    return jnp.concatenate([first_half, NBLK - first_half]).astype(jnp.int32)


def with_spikes(drawn, key, source, target, blocks, factor):
    def block_of(dim):
        return (jnp.arange(drawn.shape[dim]) // (drawn.shape[dim] // blocks)).reshape((-1,) + (1,) * (drawn.ndim - 1 - dim))

    first = jax.random.permutation(key, blocks)[block_of(target)]
    far = (block_of(target) + blocks // 2) % blocks
    return jnp.where((block_of(source) == first) | (block_of(source) == far), factor * drawn, drawn)


def shard_levels(rng, dims, split, low, top_value):
    def one(axis_at, shards_of):
        draws = jax.random.uniform(jax.random.fold_in(jax.random.fold_in(rng, 6), axis_at), (shards_of,), jnp.float32, low / len(split), top_value / len(split))
        return jnp.repeat(jnp.exp(draws), dims[axis_at] // shards_of).reshape((-1,) + (1,) * (len(dims) - axis_at - 1))

    level = one(*split[0])
    for cut in split[1:]:
        level = level * one(*cut)
    return level


def gaussian(own_key, shape, deviation, limit, cuts=(), held_as=jnp.bfloat16):
    array = deviation * jax.random.normal(own_key, shape, jnp.float32)
    if cuts:
        array = array * shard_levels(own_key, shape, cuts, -0.22, 0.18)
    return jnp.clip(array, -limit, limit).astype(held_as)


def heavy_noise(stream_key, extent, spread, reach, cuts, heavy, kind=jnp.bfloat16):
    values = spread * jax.random.normal(stream_key, extent, jnp.float32)
    if cuts:
        values = values * shard_levels(stream_key, extent, cuts, -0.22, 0.18)
    return jnp.clip(with_spikes(values, jax.random.fold_in(stream_key, 3), *heavy), -reach, reach).astype(kind)


def setup_inputs(seed: int = 0) -> dict:
    splits = jax.random.split(jax.random.key(seed), 7)
    return {
        "hidden": heavy_noise(splits[0], (TOKENS, D), 1.0, 16.0, ((0, 64), (1, 4)), (0, 1, 64, 4.0)),
        "kv_weight": gaussian(splits[1], (D, 2 * KV_HEADS * HEAD_DIM), D ** -0.5, 0.0625, ((1, 4),)),
        "queries": draw_queries(jax.random.fold_in(splits[6], 71), 0),
        "out_grad": gaussian(splits[3], (TOKENS, HEADS * HEAD_DIM), 1.0, 6.0, ((0, 64), (1, 4))),
        "live_blocks": draw_live_blocks(jax.random.fold_in(splits[6], 71), 0),
        "doc_start": draw_doc_start(jax.random.fold_in(splits[6], 71), 0),
    }


def attend_block(query_blk, key_blk, value_blk, grad_blk, start_blk, live_flag):
    factor = HEAD_DIM ** -0.5
    position = jnp.arange(BLOCK)
    allowed = (position[None, :] >= start_blk[:, None]) & (position[None, :] <= position[:, None]) & live_flag
    allowed = allowed[None, None]
    scores = jnp.einsum("rkgd,skd->kgrs", query_blk.astype(jnp.float32), key_blk.astype(jnp.float32)) * factor
    row_max = jnp.max(jnp.where(allowed, scores, -1e30), axis=-1, keepdims=True)
    weights = jnp.where(allowed, jnp.exp(scores - row_max), 0.0)
    row_sum = jnp.sum(weights, axis=-1, keepdims=True)
    row_sum = jnp.where(live_flag, row_sum, 1.0)
    prob_full = weights / row_sum
    prob_low = lax.optimization_barrier(prob_full.astype(jnp.bfloat16))
    attended = jnp.einsum("kgrs,skd->rkgd", prob_low.astype(jnp.float32), value_blk.astype(jnp.float32)).astype(jnp.bfloat16)
    attended = lax.optimization_barrier(attended)
    row_dot = jnp.sum(grad_blk.astype(jnp.float32) * attended.astype(jnp.float32), axis=-1)
    prob_grad = jnp.einsum("rkgd,skd->kgrs", grad_blk.astype(jnp.float32), value_blk.astype(jnp.float32))
    score_grad = (prob_full * (prob_grad - jnp.transpose(row_dot, (1, 2, 0))[..., None]) * factor).astype(jnp.bfloat16)
    score_grad = lax.optimization_barrier(score_grad)
    query_grad = jnp.einsum("kgrs,skd->rkgd", score_grad.astype(jnp.float32), key_blk.astype(jnp.float32)).astype(jnp.bfloat16)
    key_grad = jnp.einsum("kgrs,rkgd->skd", score_grad.astype(jnp.float32), query_blk.astype(jnp.float32)).astype(jnp.bfloat16)
    value_grad = jnp.einsum("kgrs,rkgd->skd", prob_low.astype(jnp.float32), grad_blk.astype(jnp.float32)).astype(jnp.bfloat16)
    return query_grad, jnp.stack([key_grad, value_grad], axis=2)


def reference(hidden, kv_weight, queries, out_grad, live_blocks, doc_start):
    row_total = hidden.shape[0]
    block_total = N_DP * NBLK
    group_size = HEADS // KV_HEADS
    kv_full = jnp.dot(hidden, kv_weight, preferred_element_type=jnp.float32).astype(jnp.bfloat16)
    kv_full = lax.optimization_barrier(kv_full)
    kv_split = kv_full.reshape(block_total, BLOCK, KV_HEADS, 2, HEAD_DIM)
    query_blocks = queries.reshape(block_total, BLOCK, KV_HEADS, group_size, HEAD_DIM)
    grad_blocks = out_grad.reshape(block_total, BLOCK, KV_HEADS, group_size, HEAD_DIM)
    start_blocks = doc_start.reshape(block_total, BLOCK)
    block_ids = jnp.arange(block_total, dtype=jnp.int32)
    live_flags = (block_ids % NBLK) < live_blocks[block_ids // NBLK]

    def one_block(inputs):
        return attend_block(inputs[0], inputs[1], inputs[2], inputs[3], inputs[4], inputs[5])

    query_grad, kv_grad = lax.map(one_block, (query_blocks, kv_split[:, :, :, 0], kv_split[:, :, :, 1], grad_blocks, start_blocks, live_flags))
    q_grad = query_grad.reshape(row_total, HEADS * HEAD_DIM)
    kv_grad = kv_grad.reshape(row_total, KV_HEADS * 2 * HEAD_DIM)
    kv_grad = lax.optimization_barrier(kv_grad)
    group_cols = KV_HEADS * 2 * HEAD_DIM // N_TENSOR
    summed = jnp.zeros((row_total, hidden.shape[1]), jnp.float32)
    for group_id in range(N_TENSOR):
        partial_value = lax.dot_general(kv_grad[:, group_id * group_cols:(group_id + 1) * group_cols], kv_weight[:, group_id * group_cols:(group_id + 1) * group_cols], (((1,), (1,)), ((), ())), preferred_element_type=jnp.float32)
        summed = summed + lax.optimization_barrier(partial_value.astype(jnp.bfloat16)).astype(jnp.float32)
    hidden_grad = summed.astype(jnp.bfloat16)
    weight_grad = lax.dot_general(hidden, kv_grad, (((0,), (0,)), ((), ())), preferred_element_type=jnp.float32)
    return q_grad, hidden_grad, weight_grad
```

```python
import jax
import jax.numpy as jnp
from jax import lax
from jax.experimental import pallas as pl
from jax.experimental.pallas import tpu as pltpu
from jax.sharding import PartitionSpec as P

BF16 = jnp.bfloat16
F32 = jnp.float32
HD = 128
ROWS = 512
NB = 4
NH = 8
KD = 2048
KC = 256
MESH = pl.DeviceIdType.MESH


def dot(a, b, dims):
    return lax.dot_general(a, b, (dims, ((), ())), preferred_element_type=F32)


def kernel(
    live_ref, start_ref, hid_hbm, w_hbm, q_hbm, g_hbm,
    qg_out, hg_out, wg_out,
    hid, hid_t, wts, qv, gv, qg, hg,
    own, pp, pf, ff, r_pp, r_pf, r_z, kvg,
    s_far, s_rt, s_lt, st_rt, st_lt, acc, r_rel, r_nbl, r_nbr,
    t_acc, q_relay, q_rel, q_nbl, q_nbr,
    z_acc, r_fin, out_v,
    loc, snd, rcv,
):
    counter = [0, 0]

    def new_sem(count=1):
        first = counter[0]
        counter[0] += count
        return first

    def new_loc():
        counter[1] += 1
        return loc.at[counter[1] - 1]

    dp = lax.axis_index("dp")
    j = lax.axis_index("tensor")
    zh = dp // 16
    y = (dp // 4) % 4
    x = dp % 4
    zl = j // 2
    c = j % 2
    pj = 2 * zl + 1 - c
    fz = 2 * (1 - zl)
    tf = fz + c
    tp = fz + 1 - c

    def dev(zh_, y_, x_, t_):
        return {"dp": zh_ * 16 + y_ * 4 + x_, "tensor": t_}

    partner = dev(zh, y, x, pj)
    pair_same = dev(zh, y, x, tf)
    pair_other = dev(zh, y, x, tp)
    zo = (zh + 2 * zl + 3) % 4
    oth_same = dev(zo, y, x, tf)
    oth_other = dev(zo, y, x, tp)
    right = (dev(zh, y, (x + 1) % 4, j), dev(zh, (y + 1) % 4, x, j))
    left = (dev(zh, y, (x + 3) % 4, j), dev(zh, (y + 3) % 4, x, j))
    me = (x, y)

    def rcopy(src, dst, sem, to):
        return pltpu.make_async_remote_copy(
            src_ref=src, dst_ref=dst, send_sem=snd.at[sem], recv_sem=rcv.at[sem],
            device_id=to, device_id_type=MESH,
        )

    cp_own = pltpu.make_async_copy(w_hbm.at[pl.ds(KD * j, KD), :], wts.at[j], new_loc())
    cp_own.start()
    cp_hid = pltpu.make_async_copy(hid_hbm, hid, new_loc())
    cp_hid.start()

    barrier = pltpu.get_barrier_semaphore()

    def greet(to):
        pl.semaphore_signal(barrier, inc=1, device_id=to, device_id_type=MESH)

    for to in (partner, pair_same, pair_other, oth_same, oth_other) + right + left:
        greet(to)
    for k in range(4):
        @pl.when(jnp.logical_not((zh == j) & (j == k)))
        def _():
            greet(dev(j, y, x, k))

        @pl.when(jnp.logical_not((zh == j) & (zh == k)))
        def _():
            greet(dev(k, y, x, zh))
    own_case = jnp.where(zh == j, 1, 0)
    pl.semaphore_wait(barrier, 17 - 2 * own_case)

    quarter = KD // 8
    cp_z = []
    for k in range(2):
        cd = (1 - c) if k == 0 else c
        td = fz + cd
        for h in range(2):
            to = ((pair_other, pair_same), (oth_other, oth_same))[h][k]
            off = 1024 * h + quarter * me[h]
            cp = rcopy(
                w_hbm.at[pl.ds(KD * td + off, quarter), :],
                wts.at[j, pl.ds(off, quarter), :], new_sem(), to,
            )
            cp.start()
            cp_z.append(cp)
    cp_pw = rcopy(w_hbm.at[pl.ds(KD * pj, KD), :], wts.at[j], new_sem(), partner)
    cp_pw.start()
    cp_q = pltpu.make_async_copy(q_hbm, qv, new_loc())
    cp_q.start()
    cp_g = pltpu.make_async_copy(g_hbm, gv, new_loc())
    cp_g.start()

    def proj(t, store):
        @pl.loop(0, 2)
        def _(n):
            rows = pl.ds(n * 256, 256)
            store(rows, dot(hid[rows, :], wts[t], ((1,), (0,))))

    def to_ref(ref):
        def store(rows, value):
            ref[rows, :] = value
        return store

    cp_hid.wait()
    cp_own.wait()
    proj(j, to_ref(own))

    ring = []
    for k in range(2):
        ts = (tp, tf)[k]
        for h in range(2):
            cp_z[2 * k + h].wait_recv()
            sems = [new_sem() for _ in range(4)]

            def piece(origin, lo, size, h=h, ts=ts):
                return wts.at[ts, pl.ds(1024 * h + quarter * origin + lo, size), :]

            mine = piece(me[h], 0, quarter)
            a = rcopy(mine, mine, sems[0], right[h])
            b = rcopy(mine, mine, sems[1], left[h])
            a.start()
            b.start()
            ring.append((k, h, a, b, sems, piece))
        if k == 0:
            cp_pw.wait_recv()
            proj(pj, to_ref(pp))
            cp_pp = rcopy(pp, r_pp, new_sem(), partner)
            cp_pp.start()
            for n in range(16):
                cols = slice(128 * n, 128 * n + 128)
                hid_t[cols, :] = hid[:, cols].T

    far = {0: [], 1: []}
    for k, h, a, b, sems, piece in ring:
        half = quarter // 2
        a.wait_recv()
        first = piece((me[h] + 3) % 4, 0, half)
        fa = rcopy(first, first, sems[2], right[h])
        fa.start()
        b.wait_recv()
        second = piece((me[h] + 1) % 4, half, half)
        fb = rcopy(second, second, sems[3], left[h])
        fb.start()
        far[k] += [fa, fb]

    for cp in far[0]:
        cp.wait_recv()
    proj(tp, to_ref(pf))
    cp_pf = rcopy(pf, r_pf, new_sem(), partner)
    cp_pf.start()
    for cp in far[1]:
        cp.wait_recv()
    proj(tf, to_ref(ff))
    cp_pf.wait_recv()
    z_sem = new_sem(NB)

    def block_z(b):
        rows = pl.ds(b * 128, 128)
        return rcopy(ff.at[rows, :], r_z.at[rows, :], z_sem + b, pair_same)

    @pl.loop(0, NB)
    def _(b):
        rows = pl.ds(b * 128, 128)
        ff[rows, :] = ff[rows, :] + r_pf[rows, :]
        block_z(b).start()

    cp_pp.wait_recv()
    cp_q.wait()
    cp_g.wait()
    live = live_ref[0]
    factor = HD ** -0.5
    kp_sem = new_sem(NB)
    kz_sem = new_sem(NB)
    kf_sem = new_sem(NB)

    def grad_copy(t, b, sem, to):
        ref = kvg.at[t, pl.ds(b * 128, 128), :]
        return rcopy(ref, ref, sem + b, to)

    @pl.loop(0, NB)
    def _(b):
        rows = pl.ds(b * 128, 128)
        block_z(b).wait_recv()
        kv = (own[rows, :] + r_pp[rows, :] + r_z[rows, :]).astype(BF16)
        key, val = kv[:, :HD], kv[:, HD:]
        qs = jnp.concatenate([qv[rows, HD * n:HD * n + HD] for n in range(NH)], axis=0)
        gs = jnp.concatenate([gv[rows, HD * n:HD * n + HD] for n in range(NH)], axis=0)
        start = jnp.broadcast_to(start_ref[pl.ds(b, 1), :], (128, 128)).T
        pos_u = lax.broadcasted_iota(jnp.int32, (128, 128), 1)
        pos_t = lax.broadcasted_iota(jnp.int32, (128, 128), 0)
        is_live = b < live
        lim = jnp.where(is_live, pos_t, -1)
        allowed = ((pos_u >= start) & (pos_u <= lim))[None]
        sc = (dot(qs, key, ((1,), (1,))) * factor).reshape(NH, 128, 128)
        top = jnp.max(jnp.where(allowed, sc, -1e30), axis=-1, keepdims=True)
        wt = jnp.where(allowed, jnp.exp(sc - top), 0.0)
        tot = jnp.sum(wt, axis=-1, keepdims=True)
        tot = jnp.where(is_live, tot, 1.0)
        prob = (wt * (1.0 / tot)).reshape(NH * 128, 128)
        low = prob.astype(BF16)
        att = dot(low, val, ((1,), (0,))).astype(BF16)
        rdot = jnp.sum(gs.astype(F32) * att.astype(F32), axis=-1, keepdims=True)
        pgrad = dot(gs, val, ((1,), (1,)))
        sg = (prob * (pgrad - rdot) * factor).astype(BF16)
        qgr = dot(sg, key, ((1,), (0,))).astype(BF16)
        for n in range(NH):
            qg[rows, HD * n:HD * n + HD] = qgr[128 * n:128 * n + 128, :]
        kvg[j, rows, :HD] = dot(sg, qs, ((0,), (0,))).astype(BF16)
        kvg[j, rows, HD:] = dot(low, gs, ((0,), (0,))).astype(BF16)
        grad_copy(j, b, kz_sem, pair_same).start()
        grad_copy(j, b, kp_sem, partner).start()

    cp_qo = pltpu.make_async_copy(qg, qg_out, new_loc())
    cp_qo.start()

    @pl.loop(0, NB)
    def _(b):
        grad_copy(tf, b, kz_sem, pair_same).wait_recv()
        grad_copy(tf, b, kf_sem, partner).start()

    @pl.loop(0, NB)
    def _(b):
        grad_copy(pj, b, kp_sem, partner).wait_recv()
        grad_copy(tp, b, kf_sem, partner).wait_recv()

    order = (0, 2, 1, 3)
    axis1 = {0: 0, 1: 0, 2: 1, 3: 1}

    def tiles(t, dest, lo, hi, store):
        sk, sd = (512, 128) if axis1[t] == 0 else (128, 512)

        @pl.loop(lo, hi)
        def _(k):
            row = pl.multiple_of(sk * k + sd * dest, 128)
            store(pl.ds(128 * k, 128), dot(hid_t[pl.ds(row, 128), :], kvg[t], ((1,), (0,))))

    def put(ref, t, low_=0):
        def store(rows, value):
            ref[t, rows, :] = value.astype(ref.dtype)
        return store

    p1 = {}

    def p1_far(t):
        h = axis1[t]
        tiles(t, (me[h] + 2) % 4, 0, 4, put(s_far, t))
        a = rcopy(s_far.at[t, 0:256, :], r_rel.at[t, 0:256, :], new_sem(), right[h])
        b = rcopy(s_far.at[t, 256:512, :], r_rel.at[t, 256:512, :], new_sem(), left[h])
        a.start()
        b.start()
        p1[t] = [a, b]

    def p1_direct(t):
        h = axis1[t]
        tiles(t, (me[h] + 1) % 4, 2, 4, put(s_rt, t))
        a = rcopy(s_rt.at[t, 256:512, :], r_nbl.at[t, 256:512, :], new_sem(), right[h])
        a.start()
        tiles(t, (me[h] + 3) % 4, 0, 2, put(s_lt, t))
        b = rcopy(s_lt.at[t, 0:256, :], r_nbr.at[t, 0:256, :], new_sem(), left[h])
        b.start()
        tiles(t, (me[h] + 1) % 4, 0, 2, put(st_rt, t))

        def low_rows(rows, value):
            st_lt[t, rows, :] = value

        tiles(t, (me[h] + 3) % 4, 2, 4, low_rows)
        tiles(t, me[h], 0, 4, put(acc, t))
        p1[t] += [a, b]

    def p1_relay(t):
        h = axis1[t]
        p1[t][0].wait_recv()
        s_rt[t, 0:256, :] = (st_rt[t, 0:256, :] + r_rel[t, 0:256, :].astype(F32)).astype(BF16)
        a = rcopy(s_rt.at[t, 0:256, :], r_nbl.at[t, 0:256, :], new_sem(), right[h])
        a.start()
        p1[t][1].wait_recv()
        s_lt[t, 256:512, :] = (st_lt[t, 256:512, :] + r_rel[t, 256:512, :].astype(F32)).astype(BF16)
        b = rcopy(s_lt.at[t, 256:512, :], r_nbr.at[t, 256:512, :], new_sem(), left[h])
        b.start()
        p1[t] += [a, b]

    p2 = {}

    def chunk(ref, t, k, lo, size):
        return ref.at[t, pl.ds(pl.multiple_of(128 * k + lo, 64), size), :]

    def p2_start(t):
        h = 1 - axis1[t]
        for cp in p1[t][2:]:
            cp.wait_recv()
        acc[t] = acc[t] + (r_nbl[t].astype(F32) + r_nbr[t].astype(F32))
        k2, kr, kl = (me[h] + 2) % 4, (me[h] + 1) % 4, (me[h] + 3) % 4
        cps = [
            rcopy(chunk(acc, t, k2, 0, 64), q_rel.at[t, 0:64, :], new_sem(), right[h]),
            rcopy(chunk(acc, t, k2, 64, 64), q_rel.at[t, 64:128, :], new_sem(), left[h]),
            rcopy(chunk(acc, t, kr, 64, 64), q_nbl.at[t, 64:128, :], new_sem(), right[h]),
            rcopy(chunk(acc, t, kl, 0, 64), q_nbr.at[t, 0:64, :], new_sem(), left[h]),
        ]
        for cp in cps:
            cp.start()
        p2[t] = cps

    def p2_relay(t):
        h = 1 - axis1[t]
        kr, kl = (me[h] + 1) % 4, (me[h] + 3) % 4
        p2[t][0].wait_recv()
        q_relay[t, 0:64, :] = chunk(acc, t, kr, 0, 64)[...] + q_rel[t, 0:64, :]
        a = rcopy(q_relay.at[t, 0:64, :], q_nbl.at[t, 0:64, :], new_sem(), right[h])
        a.start()
        p2[t][1].wait_recv()
        q_relay[t, 64:128, :] = chunk(acc, t, kl, 64, 64)[...] + q_rel[t, 64:128, :]
        b = rcopy(q_relay.at[t, 64:128, :], q_nbr.at[t, 64:128, :], new_sem(), left[h])
        b.start()
        p2[t] += [a, b]

    p3 = {}
    fin_sem = new_sem(4)
    fin_send = new_sem(4)

    def p3_start(t):
        h = 1 - axis1[t]
        for cp in p2[t][2:]:
            cp.wait_recv()
        z_acc[t] = chunk(acc, t, me[h], 0, 128)[...] + (q_nbl[t] + q_nbr[t])
        local = (zh == j) & (j == t)
        cp = pltpu.make_async_remote_copy(
            src_ref=z_acc.at[t], dst_ref=r_fin.at[zh],
            send_sem=snd.at[fin_send + t], recv_sem=rcv.at[fin_sem + zh],
            device_id=dev(j, y, x, t), device_id_type=MESH,
        )

        @pl.when(local)
        def _():
            r_fin[zh] = z_acc[t]

        @pl.when(jnp.logical_not(local))
        def _():
            cp.start()

        p3[t] = (local, cp)

    p1_far(0)
    p1_far(2)
    p1_direct(0)
    p1_direct(2)
    p1_far(1)
    p1_far(3)
    p1_relay(0)
    p1_relay(2)
    p1_direct(1)
    p1_direct(3)
    p1_relay(1)
    p1_relay(3)

    @pl.loop(0, KD // 256)
    def _(n):
        cols = pl.ds(pl.multiple_of(n * 256, 256), 256)
        total = jnp.zeros((ROWS, 256), F32)
        for t in range(4):
            part = dot(kvg[t], wts[t, cols, :], ((1,), (1,)))
            total = total + part.astype(BF16).astype(F32)
        hg[:, cols] = total.astype(BF16)

    cp_ho = pltpu.make_async_copy(hg, hg_out, new_loc())
    cp_ho.start()

    p2_start(0)
    p2_start(2)
    p2_relay(0)
    p2_relay(2)
    p2_start(1)
    p2_start(3)
    p3_start(0)
    p3_start(2)
    p2_relay(1)
    p2_relay(3)
    p3_start(1)
    p3_start(3)

    for k in range(4):
        @pl.when(jnp.logical_not((zh == j) & (zh == k)))
        def _():
            pltpu.make_async_remote_copy(
                src_ref=z_acc.at[k], dst_ref=r_fin.at[k],
                send_sem=snd.at[fin_send + k], recv_sem=rcv.at[fin_sem + k],
                device_id=dev(k, y, x, zh), device_id_type=MESH,
            ).wait_recv()

    out_v[...] = (r_fin[0] + r_fin[1]) + (r_fin[2] + r_fin[3])
    cp_wo = pltpu.make_async_copy(out_v, wg_out, new_loc())
    cp_wo.start()

    for cp in cp_z:
        cp.wait_send()
    for cp in (cp_pw, cp_pp, cp_pf):
        cp.wait_send()
    for k, h, a, b, sems, piece in ring:
        a.wait_send()
        b.wait_send()
    for cp in far[0] + far[1]:
        cp.wait_send()

    @pl.loop(0, NB)
    def _(b):
        block_z(b).wait_send()
        grad_copy(j, b, kz_sem, pair_same).wait_send()
        grad_copy(j, b, kp_sem, partner).wait_send()
        grad_copy(tf, b, kf_sem, partner).wait_send()

    for t in range(4):
        for cp in p1[t] + p2[t]:
            cp.wait_send()
        local, cp = p3[t]

        @pl.when(jnp.logical_not(local))
        def _():
            cp.wait_send()

    cp_qo.wait()
    cp_ho.wait()
    cp_wo.wait()


N_SEM = 160
N_LOC = 8


def on_device(hidden, kv_weight, queries, out_grad, live_blocks, doc_start):
    any_ = pl.BlockSpec(memory_space=pl.ANY)
    vm = pltpu.VMEM
    return pl.pallas_call(
        kernel,
        out_shape=(
            jax.ShapeDtypeStruct((ROWS, NH * HD), BF16),
            jax.ShapeDtypeStruct((ROWS, KD), BF16),
            jax.ShapeDtypeStruct((128, KC), F32),
        ),
        in_specs=[
            pl.BlockSpec(memory_space=pltpu.SMEM),
            pl.BlockSpec(memory_space=pltpu.VMEM),
            any_, any_, any_, any_,
        ],
        out_specs=(any_, any_, any_),
        scratch_shapes=[
            vm((ROWS, KD), BF16), vm((KD, ROWS), BF16), vm((4, KD, KC), BF16),
            vm((ROWS, NH * HD), BF16), vm((ROWS, NH * HD), BF16), vm((ROWS, NH * HD), BF16),
            vm((ROWS, KD), BF16),
            vm((ROWS, KC), F32), vm((ROWS, KC), F32), vm((ROWS, KC), F32), vm((ROWS, KC), F32),
            vm((ROWS, KC), F32), vm((ROWS, KC), F32), vm((ROWS, KC), F32),
            vm((4, ROWS, KC), BF16),
            vm((4, ROWS, KC), BF16), vm((4, ROWS, KC), BF16), vm((4, ROWS, KC), BF16),
            vm((4, ROWS, KC), F32), vm((4, ROWS, KC), F32), vm((4, ROWS, KC), F32),
            vm((4, ROWS, KC), BF16), vm((4, ROWS, KC), BF16), vm((4, ROWS, KC), BF16),
            vm((8, 128), F32),
            vm((4, 128, KC), F32), vm((4, 128, KC), F32), vm((4, 128, KC), F32), vm((4, 128, KC), F32),
            vm((4, 128, KC), F32), vm((4, 128, KC), F32), vm((128, KC), F32),
            pltpu.SemaphoreType.DMA((N_LOC,)),
            pltpu.SemaphoreType.DMA((N_SEM,)),
            pltpu.SemaphoreType.DMA((N_SEM,)),
        ],
        compiler_params=pltpu.CompilerParams(
            collective_id=0, has_side_effects=True, vmem_limit_bytes=60 * 1024 * 1024
        ),
        name="fused_step",
    )(live_blocks, doc_start.reshape(NB, 128), hidden, kv_weight, queries, out_grad)


def solution(mesh):
    in_specs = (
        P("dp", "tensor"),
        P(None, "tensor"),
        P("dp", "tensor"),
        P("dp", "tensor"),
        P("dp"),
        P("dp"),
    )
    out_specs = (P("dp", "tensor"), P("dp", "tensor"), P("dp", "tensor"))
    return jax.shard_map(
        on_device, mesh=mesh, in_specs=in_specs, out_specs=out_specs, check_vma=False
    )
```

```python
import jax
import jax.numpy as jnp
from jax import lax
from jax.experimental import pallas as pl
from jax.experimental.pallas import tpu as pltpu
from jax.sharding import PartitionSpec as P

BF16 = jnp.bfloat16
F32 = jnp.float32
HD = 128
ROWS = 512
NB = 4
NH = 8
KD = 2048
KC = 256
MESH = pl.DeviceIdType.MESH


def dot(a, b, dims):
    return lax.dot_general(a, b, (dims, ((), ())), preferred_element_type=F32)


def kernel(
    live_ref, start_ref, hid_hbm, w_hbm, q_hbm, g_hbm,
    qg, hg, wg_out,
    hid, hid_t, wts, qv, gv,
    own, pp, pf, ff, r_pp, r_pf, r_z, kvg,
    s_far, s_rt, s_lt, st_rt, st_lt, acc, r_rel, r_nbl, r_nbr,
    q_relay, q_rel, q_nbl, q_nbr,
    z_acc, r_fin,
    loc, snd, rcv,
):
    counter = [0, 0]

    def new_sem(count=1):
        first = counter[0]
        counter[0] += count
        return first

    def new_loc():
        counter[1] += 1
        return loc.at[counter[1] - 1]

    dp = lax.axis_index("dp")
    j = lax.axis_index("tensor")
    zh = dp // 16
    y = (dp // 4) % 4
    x = dp % 4
    zl = j // 2
    c = j % 2
    pj = 2 * zl + 1 - c
    fz = 2 * (1 - zl)
    tf = fz + c
    tp = fz + 1 - c

    def dev(zh_, y_, x_, t_):
        return {"dp": zh_ * 16 + y_ * 4 + x_, "tensor": t_}

    partner = dev(zh, y, x, pj)
    pair_same = dev(zh, y, x, tf)
    pair_other = dev(zh, y, x, tp)
    zo = (zh + 2 * zl + 3) % 4
    oth_same = dev(zo, y, x, tf)
    oth_other = dev(zo, y, x, tp)
    right = (dev(zh, y, (x + 1) % 4, j), dev(zh, (y + 1) % 4, x, j))
    left = (dev(zh, y, (x + 3) % 4, j), dev(zh, (y + 3) % 4, x, j))
    me = (x, y)

    sent = []

    def finish():
        for wait in sent:
            wait()

    def rcopy(src, dst, sem, to, keep=True):
        cp = pltpu.make_async_remote_copy(
            src_ref=src, dst_ref=dst, send_sem=snd.at[sem], recv_sem=rcv.at[sem],
            device_id=to, device_id_type=MESH,
        )
        if keep:
            sent.append(cp.wait_send)
        return cp

    def looped(make):
        def wait():
            @pl.loop(0, NB)
            def _(b):
                make(b).wait_send()

        sent.append(wait)

    cp_own = pltpu.make_async_copy(w_hbm.at[pl.ds(KD * j, KD), :], wts.at[j], new_loc())
    cp_own.start()
    cp_hid = pltpu.make_async_copy(hid_hbm, hid, new_loc())
    cp_hid.start()

    barrier = pltpu.get_barrier_semaphore()

    def greet(to):
        pl.semaphore_signal(barrier, inc=1, device_id=to, device_id_type=MESH)

    for to in (partner, pair_same, pair_other, oth_same, oth_other) + right + left:
        greet(to)
    for k in range(4):
        @pl.when(jnp.logical_not((zh == j) & (j == k)))
        def _():
            greet(dev(j, y, x, k))

        @pl.when(jnp.logical_not((zh == j) & (zh == k)))
        def _():
            greet(dev(k, y, x, zh))
    own_case = jnp.where(zh == j, 1, 0)
    pl.semaphore_wait(barrier, 17 - 2 * own_case)

    quarter = KD // 8
    piece_rows = quarter // 2
    cp_z = {}
    for k in range(2):
        cd = (1 - c) if k == 0 else c
        td = fz + cd
        for n in range(2):
            for h in range(2):
                to = ((pair_other, pair_same), (oth_other, oth_same))[h][k]
                off = 1024 * h + quarter * me[h] + piece_rows * n
                cp = rcopy(
                    w_hbm.at[pl.ds(KD * td + off, piece_rows), :],
                    wts.at[j, pl.ds(off, piece_rows), :], new_sem(), to,
                )
                cp.start()
                cp_z[k, n, h] = cp
    cp_pw = rcopy(w_hbm.at[pl.ds(KD * pj, KD), :], wts.at[j], new_sem(), partner)
    cp_pw.start()
    cp_q = pltpu.make_async_copy(q_hbm, qv, new_loc())
    cp_q.start()
    cp_g = pltpu.make_async_copy(g_hbm, gv, new_loc())
    cp_g.start()

    def proj(t, store):
        @pl.loop(0, 2)
        def _(n):
            rows = pl.ds(n * 256, 256)
            store(rows, dot(hid[rows, :], wts[t], ((1,), (0,))))

    def to_ref(ref):
        def store(rows, value):
            ref[rows, :] = value
        return store

    ring = {}

    def ring_near(k):
        ts = (tp, tf)[k]
        for n in range(2):
            for h in range(2):
                cp_z[k, n, h].wait_recv()
                sems = [new_sem() for _ in range(4)]

                def piece(origin, lo, size, h=h, ts=ts, n=n):
                    off = 1024 * h + quarter * origin + piece_rows * n + lo
                    return wts.at[ts, pl.ds(off, size), :]

                mine = piece(me[h], 0, piece_rows)
                a = rcopy(mine, mine, sems[0], right[h])
                b = rcopy(mine, mine, sems[1], left[h])
                a.start()
                b.start()
                ring[k, n, h] = (a, b, sems, piece)

    far = {0: [], 1: []}

    def ring_far(k):
        half = piece_rows // 2
        for n in range(2):
            for h in range(2):
                a, b, sems, piece = ring[k, n, h]
                a.wait_recv()
                first = piece((me[h] + 3) % 4, 0, half)
                fa = rcopy(first, first, sems[2], right[h])
                fa.start()
                b.wait_recv()
                second = piece((me[h] + 1) % 4, half, half)
                fb = rcopy(second, second, sems[3], left[h])
                fb.start()
                far[k] += [fa, fb]

    ring_near(0)
    cp_hid.wait()
    cp_own.wait()
    proj(j, to_ref(own))
    ring_near(1)
    ring_far(0)
    cp_pw.wait_recv()
    proj(pj, to_ref(pp))
    cp_pp = rcopy(pp, r_pp, new_sem(), partner)
    cp_pp.start()
    ring_far(1)

    for cp in far[0]:
        cp.wait_recv()
    proj(tp, to_ref(pf))
    cp_pf = rcopy(pf, r_pf, new_sem(), partner)
    cp_pf.start()
    for cp in far[1]:
        cp.wait_recv()
    proj(tf, to_ref(ff))
    cp_pf.wait_recv()
    z_sem = new_sem(NB)

    def block_z(b):
        rows = pl.ds(b * 128, 128)
        return rcopy(ff.at[rows, :], r_z.at[rows, :], z_sem + b, pair_same, keep=False)

    @pl.loop(0, NB)
    def _(b):
        rows = pl.ds(b * 128, 128)
        ff[rows, :] = ff[rows, :] + r_pf[rows, :]
        block_z(b).start()

    looped(block_z)
    cp_pp.wait_recv()
    cp_q.wait()
    cp_g.wait()
    live = live_ref[0]
    factor = HD ** -0.5
    kp_sem = new_sem(NB)
    kz_sem = new_sem(NB)
    kf_sem = new_sem(NB)

    def grad_copy(t, b, sem, to):
        ref = kvg.at[t, pl.ds(b * 128, 128), :]
        return rcopy(ref, ref, sem + b, to, keep=False)

    @pl.loop(0, NB)
    def _(b):
        rows = pl.ds(b * 128, 128)
        for n in range(4):
            cols = pl.ds(pl.multiple_of(512 * b + 128 * n, 128), 128)
            hid_t[cols, :] = hid[:, cols].T
        block_z(b).wait_recv()
        kv = (own[rows, :] + r_pp[rows, :] + r_z[rows, :]).astype(BF16)
        key, val = kv[:, :HD], kv[:, HD:]
        qs = jnp.concatenate([qv[rows, HD * n:HD * n + HD] for n in range(NH)], axis=0)
        gs = jnp.concatenate([gv[rows, HD * n:HD * n + HD] for n in range(NH)], axis=0)
        start = jnp.broadcast_to(start_ref[pl.ds(b, 1), :], (128, 128)).T
        pos_u = lax.broadcasted_iota(jnp.int32, (128, 128), 1)
        pos_t = lax.broadcasted_iota(jnp.int32, (128, 128), 0)
        is_live = b < live
        lim = jnp.where(is_live, pos_t, -1)
        allowed = ((pos_u >= start) & (pos_u <= lim))[None]
        sc = (dot(qs, key, ((1,), (1,))) * factor).reshape(NH, 128, 128)
        top = jnp.max(jnp.where(allowed, sc, -1e30), axis=-1, keepdims=True)
        wt = jnp.where(allowed, jnp.exp(sc - top), 0.0)
        tot = jnp.sum(wt, axis=-1, keepdims=True)
        tot = jnp.where(is_live, tot, 1.0)
        prob = (wt * (1.0 / tot)).reshape(NH * 128, 128)
        low = prob.astype(BF16)
        att = dot(low, val, ((1,), (0,))).astype(BF16)
        rdot = jnp.sum(gs.astype(F32) * att.astype(F32), axis=-1, keepdims=True)
        pgrad = dot(gs, val, ((1,), (1,)))
        sg = (prob * (pgrad - rdot) * factor).astype(BF16)
        qgr = dot(sg, key, ((1,), (0,))).astype(BF16)
        for n in range(NH):
            qg[rows, HD * n:HD * n + HD] = qgr[128 * n:128 * n + 128, :]
        kvg[j, rows, :HD] = dot(sg, qs, ((0,), (0,))).astype(BF16)
        kvg[j, rows, HD:] = dot(low, gs, ((0,), (0,))).astype(BF16)
        grad_copy(j, b, kz_sem, pair_same).start()
        grad_copy(j, b, kp_sem, partner).start()

    looped(lambda b: grad_copy(j, b, kz_sem, pair_same))
    looped(lambda b: grad_copy(j, b, kp_sem, partner))
    @pl.loop(0, NB)
    def _(b):
        grad_copy(tf, b, kz_sem, pair_same).wait_recv()
        grad_copy(tf, b, kf_sem, partner).start()

    looped(lambda b: grad_copy(tf, b, kf_sem, partner))

    @pl.loop(0, NB)
    def _(b):
        grad_copy(pj, b, kp_sem, partner).wait_recv()
        grad_copy(tp, b, kf_sem, partner).wait_recv()

    axis1 = (0, 0, 1, 1)
    jobs = ((0, 0), (2, 0), (0, 1), (2, 1), (1, 0), (3, 0), (1, 1), (3, 1))

    def partial(i, dest):
        t, s = jobs[i]
        sk, sd = (512, 128) if axis1[t] == 0 else (128, 512)
        lhs = [
            hid_t[pl.ds(pl.multiple_of(sk * k + sd * dest + 64 * s, 64), 64), :]
            for k in range(4)
        ]
        return dot(jnp.concatenate(lhs, axis=0), kvg[t], ((1,), (0,)))

    lo, hi = slice(0, 128), slice(128, 256)
    p1 = {}

    def p1_far(i):
        h = axis1[jobs[i][0]]
        s_far[i] = partial(i, (me[h] + 2) % 4).astype(BF16)
        a = rcopy(s_far.at[i, lo, :], r_rel.at[i, lo, :], new_sem(), right[h])
        b = rcopy(s_far.at[i, hi, :], r_rel.at[i, hi, :], new_sem(), left[h])
        a.start()
        b.start()
        p1[i] = [a, b]

    def p1_direct(i):
        h = axis1[jobs[i][0]]
        part = partial(i, (me[h] + 1) % 4)
        s_rt[i, hi, :] = part[hi, :].astype(BF16)
        st_rt[i] = part[lo, :]
        a = rcopy(s_rt.at[i, hi, :], r_nbl.at[i, hi, :], new_sem(), right[h])
        a.start()
        part = partial(i, (me[h] + 3) % 4)
        s_lt[i, lo, :] = part[lo, :].astype(BF16)
        st_lt[i] = part[hi, :]
        b = rcopy(s_lt.at[i, lo, :], r_nbr.at[i, lo, :], new_sem(), left[h])
        b.start()
        p1[i] += [a, b]

    def p1_own(i):
        acc[i] = partial(i, me[axis1[jobs[i][0]]])

    def p1_relay(i):
        h = axis1[jobs[i][0]]
        p1[i][0].wait_recv()
        s_rt[i, lo, :] = (st_rt[i] + r_rel[i, lo, :].astype(F32)).astype(BF16)
        a = rcopy(s_rt.at[i, lo, :], r_nbl.at[i, lo, :], new_sem(), right[h])
        a.start()
        p1[i][1].wait_recv()
        s_lt[i, hi, :] = (st_lt[i] + r_rel[i, hi, :].astype(F32)).astype(BF16)
        b = rcopy(s_lt.at[i, hi, :], r_nbr.at[i, hi, :], new_sem(), left[h])
        b.start()
        p1[i] += [a, b]

    p2 = {}

    def chunk(i, k, low, size):
        return acc.at[i, pl.ds(pl.multiple_of(64 * k + low, 32), size), :]

    def p2_start(i):
        h = 1 - axis1[jobs[i][0]]
        for cp in p1[i][2:]:
            cp.wait_recv()
        acc[i] = acc[i] + (r_nbl[i].astype(F32) + r_nbr[i].astype(F32))
        k2, kr, kl = (me[h] + 2) % 4, (me[h] + 1) % 4, (me[h] + 3) % 4
        cps = [
            rcopy(chunk(i, k2, 0, 32), q_rel.at[i, 0:32, :], new_sem(), right[h]),
            rcopy(chunk(i, k2, 32, 32), q_rel.at[i, 32:64, :], new_sem(), left[h]),
            rcopy(chunk(i, kr, 32, 32), q_nbl.at[i, 32:64, :], new_sem(), right[h]),
            rcopy(chunk(i, kl, 0, 32), q_nbr.at[i, 0:32, :], new_sem(), left[h]),
        ]
        for cp in cps:
            cp.start()
        p2[i] = cps

    def p2_relay(i):
        h = 1 - axis1[jobs[i][0]]
        kr, kl = (me[h] + 1) % 4, (me[h] + 3) % 4
        p2[i][0].wait_recv()
        q_relay[i, 0:32, :] = chunk(i, kr, 0, 32)[...] + q_rel[i, 0:32, :]
        a = rcopy(q_relay.at[i, 0:32, :], q_nbl.at[i, 0:32, :], new_sem(), right[h])
        a.start()
        p2[i][1].wait_recv()
        q_relay[i, 32:64, :] = chunk(i, kl, 32, 32)[...] + q_rel[i, 32:64, :]
        b = rcopy(q_relay.at[i, 32:64, :], q_nbr.at[i, 32:64, :], new_sem(), left[h])
        b.start()
        p2[i] += [a, b]

    fin_send = new_sem(8)
    fin_recv = new_sem(8)

    def fin_copy(t, s, source, to):
        rows = pl.ds(64 * s, 64)
        return pltpu.make_async_remote_copy(
            src_ref=z_acc.at[t, rows, :], dst_ref=r_fin.at[source, rows, :],
            send_sem=snd.at[fin_send + 2 * t + s], recv_sem=rcv.at[fin_recv + 2 * source + s],
            device_id=to, device_id_type=MESH,
        )

    def p3_start(i):
        t, s = jobs[i]
        h = 1 - axis1[t]
        for cp in p2[i][2:]:
            cp.wait_recv()
        rows = pl.ds(64 * s, 64)
        z_acc[t, rows, :] = chunk(i, me[h], 0, 64)[...] + (q_nbl[i] + q_nbr[i])
        local = (zh == j) & (j == t)
        cp = fin_copy(t, s, zh, dev(j, y, x, t))

        @pl.when(local)
        def _():
            r_fin[zh, rows, :] = z_acc[t, rows, :]

        @pl.when(jnp.logical_not(local))
        def _():
            cp.start()

        @sent.append
        def _():
            @pl.when(jnp.logical_not(local))
            def _():
                cp.wait_send()

    def both(f, n):
        f(2 * n)
        f(2 * n + 1)

    def hidden_grad(first, last):
        @pl.loop(first, last)
        def _(n):
            cols = pl.ds(pl.multiple_of(n * 256, 256), 256)
            total = jnp.zeros((ROWS, 256), F32)
            for t in range(4):
                part = dot(kvg[t], wts[t, cols, :], ((1,), (1,)))
                total = total + part.astype(BF16).astype(F32)
            hg[:, cols] = total.astype(BF16)

    both(p1_far, 0)
    both(p1_direct, 0)
    both(p1_far, 1)
    both(p1_own, 0)
    both(p1_relay, 0)
    both(p1_direct, 1)
    both(p1_far, 2)
    both(p1_own, 1)
    both(p1_relay, 1)
    both(p1_direct, 2)
    both(p2_start, 0)
    both(p1_far, 3)
    both(p1_relay, 2)
    both(p2_relay, 0)
    both(p1_direct, 3)
    both(p1_own, 2)
    both(p1_own, 3)
    both(p2_start, 1)
    both(p3_start, 0)
    both(p1_relay, 3)
    both(p2_relay, 1)
    hidden_grad(0, 3)
    both(p2_start, 2)
    both(p3_start, 1)
    both(p2_relay, 2)
    hidden_grad(3, 6)
    both(p2_start, 3)
    both(p3_start, 2)
    both(p2_relay, 3)
    hidden_grad(6, 8)
    both(p3_start, 3)
    for k in range(4):
        @pl.when(jnp.logical_not((zh == j) & (zh == k)))
        def _():
            for s in range(2):
                fin_copy(k, s, k, dev(k, y, x, zh)).wait_recv()

    wg_out[...] = (r_fin[0] + r_fin[1]) + (r_fin[2] + r_fin[3])
    finish()


N_SEM = 192
N_LOC = 8


def leave(qg, hg, wg, qg_out, hg_out, wg_out, sems):
    cps = [
        pltpu.make_async_copy(src, dst, sems.at[n])
        for n, (src, dst) in enumerate(((hg, hg_out), (qg, qg_out), (wg, wg_out)))
    ]
    for cp in cps:
        cp.start()
    for cp in cps:
        cp.wait()


def on_device(hidden, kv_weight, queries, out_grad, live_blocks, doc_start):
    any_ = pl.BlockSpec(memory_space=pl.ANY)
    vmem = pl.BlockSpec(memory_space=pltpu.VMEM)
    vm = pltpu.VMEM
    results = ((ROWS, NH * HD), BF16), ((ROWS, KD), BF16), ((128, KC), F32)
    fused = pl.pallas_call(
        kernel,
        out_shape=tuple(vm(*r) for r in results),
        in_specs=[pl.BlockSpec(memory_space=pltpu.SMEM), vmem, any_, any_, any_, any_],
        out_specs=(vmem, vmem, vmem),
        scratch_shapes=[
            vm((ROWS, KD), BF16), vm((KD, ROWS), BF16), vm((4, KD, KC), BF16),
            vm((ROWS, NH * HD), BF16), vm((ROWS, NH * HD), BF16),
            vm((ROWS, KC), F32), vm((ROWS, KC), F32), vm((ROWS, KC), F32), vm((ROWS, KC), F32),
            vm((ROWS, KC), F32), vm((ROWS, KC), F32), vm((ROWS, KC), F32),
            vm((4, ROWS, KC), BF16),
            vm((8, 256, KC), BF16), vm((8, 256, KC), BF16), vm((8, 256, KC), BF16),
            vm((8, 128, KC), F32), vm((8, 128, KC), F32), vm((8, 256, KC), F32),
            vm((8, 256, KC), BF16), vm((8, 256, KC), BF16), vm((8, 256, KC), BF16),
            vm((8, 64, KC), F32), vm((8, 64, KC), F32), vm((8, 64, KC), F32), vm((8, 64, KC), F32),
            vm((4, 128, KC), F32), vm((4, 128, KC), F32),
            pltpu.SemaphoreType.DMA((N_LOC,)),
            pltpu.SemaphoreType.DMA((N_SEM,)),
            pltpu.SemaphoreType.DMA((N_SEM,)),
        ],
        compiler_params=pltpu.CompilerParams(
            collective_id=0, has_side_effects=True, vmem_limit_bytes=58 * 1024 * 1024
        ),
        name="fused_step",
    )(live_blocks, doc_start.reshape(NB, 128), hidden, kv_weight, queries, out_grad)
    return pl.pallas_call(
        leave,
        out_shape=tuple(jax.ShapeDtypeStruct(*r) for r in results),
        in_specs=[vmem, vmem, vmem],
        out_specs=(any_, any_, any_),
        scratch_shapes=[pltpu.SemaphoreType.DMA((3,))],
        compiler_params=pltpu.CompilerParams(vmem_limit_bytes=1024 * 1024),
        name="leave",
    )(*fused)


def solution(mesh):
    in_specs = (
        P("dp", "tensor"),
        P(None, "tensor"),
        P("dp", "tensor"),
        P("dp", "tensor"),
        P("dp"),
        P("dp"),
    )
    out_specs = (P("dp", "tensor"), P("dp", "tensor"), P("dp", "tensor"))
    return jax.shard_map(
        on_device, mesh=mesh, in_specs=in_specs, out_specs=out_specs, check_vma=False
    )
```

```python
import jax
import jax.numpy as jnp
from jax import lax
from jax.experimental import pallas as pl
from jax.experimental.pallas import tpu as pltpu
from jax.sharding import PartitionSpec as P

BF16 = jnp.bfloat16
F32 = jnp.float32
HD = 128
ROWS = 512
NB = 4
NH = 8
KD = 2048
KC = 256
MESH = pl.DeviceIdType.MESH


def dot(a, b, dims):
    return lax.dot_general(a, b, (dims, ((), ())), preferred_element_type=F32)


def kernel(
    live_ref, start_ref, hid_hbm, w_hbm, q_hbm, g_hbm,
    qg, hg, wg_out,
    hid, hid_t, wts, qv, gv,
    own, pp, pf, ff, r_pp, r_pf, r_z, kvg,
    hx, kx, acc, s_far, s_rt, s_lt, q_far, q_nbl, q_nbr,
    z_acc, r_fin,
    loc, snd, rcv,
):
    counter = [0, 0]

    def new_sem(count=1):
        first = counter[0]
        counter[0] += count
        return first

    def new_loc():
        counter[1] += 1
        return loc.at[counter[1] - 1]

    dp = lax.axis_index("dp")
    j = lax.axis_index("tensor")
    zh = dp // 16
    y = (dp // 4) % 4
    x = dp % 4
    zl = j // 2
    c = j % 2
    pj = 2 * zl + 1 - c
    fz = 2 * (1 - zl)
    tf = fz + c
    tp = fz + 1 - c

    def dev(zh_, y_, x_, t_):
        return {"dp": zh_ * 16 + y_ * 4 + x_, "tensor": t_}

    partner = dev(zh, y, x, pj)
    pair_same = dev(zh, y, x, tf)
    pair_other = dev(zh, y, x, tp)
    zo = (zh + 2 * zl + 3) % 4
    oth_same = dev(zo, y, x, tf)
    oth_other = dev(zo, y, x, tp)
    right = (dev(zh, y, (x + 1) % 4, j), dev(zh, (y + 1) % 4, x, j))
    left = (dev(zh, y, (x + 3) % 4, j), dev(zh, (y + 3) % 4, x, j))
    across = (dev(zh, y, (x + 2) % 4, j), dev(zh, (y + 2) % 4, x, j))
    me = (x, y)

    sent = []

    def finish():
        for wait in sent:
            wait()

    def rcopy(src, dst, sem, to, keep=True):
        cp = pltpu.make_async_remote_copy(
            src_ref=src, dst_ref=dst, send_sem=snd.at[sem], recv_sem=rcv.at[sem],
            device_id=to, device_id_type=MESH,
        )
        if keep:
            sent.append(cp.wait_send)
        return cp

    def looped(make):
        def wait():
            @pl.loop(0, NB)
            def _(b):
                make(b).wait_send()

        sent.append(wait)

    cp_own = pltpu.make_async_copy(w_hbm.at[pl.ds(KD * j, KD), :], wts.at[j], new_loc())
    cp_own.start()
    cp_hid = pltpu.make_async_copy(hid_hbm, hid, new_loc())
    cp_hid.start()

    barrier = pltpu.get_barrier_semaphore()

    def greet(to):
        pl.semaphore_signal(barrier, inc=1, device_id=to, device_id_type=MESH)

    for to in (partner, pair_same, pair_other, oth_same, oth_other) + right + left + across:
        greet(to)
    for k in range(4):
        @pl.when(jnp.logical_not((zh == j) & (j == k)))
        def _():
            greet(dev(j, y, x, k))

        @pl.when(jnp.logical_not((zh == j) & (zh == k)))
        def _():
            greet(dev(k, y, x, zh))
    own_case = jnp.where(zh == j, 1, 0)
    pl.semaphore_wait(barrier, 19 - 2 * own_case)

    quarter = KD // 8
    piece_rows = quarter // 2
    cp_z = {}
    for k in range(2):
        cd = (1 - c) if k == 0 else c
        td = fz + cd
        for n in range(2):
            for h in range(2):
                to = ((pair_other, pair_same), (oth_other, oth_same))[h][k]
                off = 1024 * h + quarter * me[h] + piece_rows * n
                cp = rcopy(
                    w_hbm.at[pl.ds(KD * td + off, piece_rows), :],
                    wts.at[j, pl.ds(off, piece_rows), :], new_sem(), to,
                )
                cp.start()
                cp_z[k, n, h] = cp
    cp_pw = rcopy(w_hbm.at[pl.ds(KD * pj, KD), :], wts.at[j], new_sem(), partner)
    cp_pw.start()
    cp_q = pltpu.make_async_copy(q_hbm, qv, new_loc())
    cp_q.start()
    cp_g = pltpu.make_async_copy(g_hbm, gv, new_loc())
    cp_g.start()

    def proj(t, store):
        @pl.loop(0, 2)
        def _(n):
            rows = pl.ds(n * 256, 256)
            store(rows, dot(hid[rows, :], wts[t], ((1,), (0,))))

    def to_ref(ref):
        def store(rows, value):
            ref[rows, :] = value
        return store

    ring = {}

    def ring_near(k):
        ts = (tp, tf)[k]
        for n in range(2):
            for h in range(2):
                cp_z[k, n, h].wait_recv()
                sems = [new_sem() for _ in range(4)]

                def piece(origin, lo, size, h=h, ts=ts, n=n):
                    off = 1024 * h + quarter * origin + piece_rows * n + lo
                    return wts.at[ts, pl.ds(off, size), :]

                mine = piece(me[h], 0, piece_rows)
                a = rcopy(mine, mine, sems[0], right[h])
                b = rcopy(mine, mine, sems[1], left[h])
                a.start()
                b.start()
                ring[k, n, h] = (a, b, sems, piece)

    far = {0: [], 1: []}

    def ring_far(k):
        half = piece_rows // 2
        for n in range(2):
            for h in range(2):
                a, b, sems, piece = ring[k, n, h]
                a.wait_recv()
                first = piece((me[h] + 3) % 4, 0, half)
                fa = rcopy(first, first, sems[2], right[h])
                fa.start()
                b.wait_recv()
                second = piece((me[h] + 1) % 4, half, half)
                fb = rcopy(second, second, sems[3], left[h])
                fb.start()
                far[k] += [fa, fb]

    cp_hid.wait()

    @pl.loop(0, 4)
    def _(k):
        for n in range(4):
            cols = pl.ds(pl.multiple_of(512 * k + 128 * n, 128), 128)
            hid_t[k, n] = hid[:, cols].T

    def block_rows(h, step):
        dest = (me[h] + step) % 4
        return hid_t.at[:, dest] if h == 0 else hid_t.at[dest]

    h_near, h_far = [], []

    def send_hidden(first, size):
        for h in range(2):
            for slot, step, to in ((0, 1, right[h]), (1, 3, left[h])):
                part = pl.ds(first, size)
                cp = rcopy(block_rows(h, step).at[part], hx.at[h, slot, part], new_sem(), to)
                cp.start()
                h_near.append(cp)

    def send_hidden_rest():
        send_hidden(2, 2)
        for h in range(2):
            cp = rcopy(block_rows(h, 2), hx.at[h, 2], new_sem(), across[h])
            cp.start()
            h_far.append(cp)

    send_hidden(0, 2)
    ring_near(0)
    cp_own.wait()
    proj(j, to_ref(own))
    ring_near(1)
    ring_far(0)
    cp_pw.wait_recv()
    proj(pj, to_ref(pp))
    cp_pp = rcopy(pp, r_pp, new_sem(), partner)
    cp_pp.start()

    ring_far(1)
    send_hidden_rest()

    for cp in far[0]:
        cp.wait_recv()
    proj(tp, to_ref(pf))
    cp_pf = rcopy(pf, r_pf, new_sem(), partner)
    cp_pf.start()
    for cp in far[1]:
        cp.wait_recv()
    proj(tf, to_ref(ff))
    cp_pf.wait_recv()
    z_sem = new_sem(NB)

    def block_z(b):
        rows = pl.ds(b * 128, 128)
        return rcopy(ff.at[rows, :], r_z.at[rows, :], z_sem + b, pair_same, keep=False)

    @pl.loop(0, NB)
    def _(b):
        rows = pl.ds(b * 128, 128)
        ff[rows, :] = ff[rows, :] + r_pf[rows, :]
        block_z(b).start()

    looped(block_z)
    cp_pp.wait_recv()
    cp_q.wait()
    cp_g.wait()
    live = live_ref[0]
    factor = HD ** -0.5
    kp_sem = new_sem(NB)
    kz_sem = new_sem(NB)
    kf_sem = new_sem(NB)

    def grad_copy(t, b, sem, to):
        ref = kvg.at[t, pl.ds(b * 128, 128), :]
        return rcopy(ref, ref, sem + b, to, keep=False)

    near_sem = [[new_sem(NB), new_sem(NB)] for _ in range(2)]
    far_sem = [new_sem(NB) for _ in range(2)]
    share_sem = [[new_sem(NB) for _ in range(3)] for _ in range(2)]
    group = (j, tf)

    def near(h, slot, b):
        rows = pl.ds(b * 128, 128)
        return rcopy(
            kvg.at[group[h], rows, :], kx.at[h, slot, c, rows, :], near_sem[h][slot] + b,
            (right, left)[slot][h], keep=False,
        )

    def far_on(h, b):
        rows = pl.ds(b * 128, 128)
        return rcopy(
            kvg.at[group[h], rows, :], kx.at[h, 2, c, rows, :], far_sem[h] + b,
            across[h], keep=False,
        )

    def spread(h, b):
        near(h, 0, b).start()
        near(h, 1, b).start()
        far_on(h, b).start()

    def share(h, slot, b, g):
        ref = kx.at[h, slot, g, pl.ds(b * 128, 128), :]
        return rcopy(ref, ref, share_sem[h][slot] + b, partner, keep=False)

    def collect(h, b):
        near(h, 0, b).wait_recv()
        share(h, 0, b, c).start()
        near(h, 1, b).wait_recv()
        share(h, 1, b, c).start()
        far_on(h, b).wait_recv()
        share(h, 2, b, c).start()

    def pass_z(b):
        grad_copy(tf, b, kz_sem, pair_same).wait_recv()
        spread(1, b)
        grad_copy(tf, b, kf_sem, partner).start()

    @pl.loop(0, NB)
    def _(b):
        rows = pl.ds(b * 128, 128)
        block_z(b).wait_recv()
        kv = (own[rows, :] + r_pp[rows, :] + r_z[rows, :]).astype(BF16)
        key, val = kv[:, :HD], kv[:, HD:]
        qs = jnp.concatenate([qv[rows, HD * n:HD * n + HD] for n in range(NH)], axis=0)
        gs = jnp.concatenate([gv[rows, HD * n:HD * n + HD] for n in range(NH)], axis=0)
        start = jnp.broadcast_to(start_ref[pl.ds(b, 1), :], (128, 128)).T
        pos_u = lax.broadcasted_iota(jnp.int32, (128, 128), 1)
        pos_t = lax.broadcasted_iota(jnp.int32, (128, 128), 0)
        is_live = b < live
        lim = jnp.where(is_live, pos_t, -1)
        allowed = ((pos_u >= start) & (pos_u <= lim))[None]
        sc = (dot(qs, key, ((1,), (1,))) * factor).reshape(NH, 128, 128)
        top = jnp.max(jnp.where(allowed, sc, -1e30), axis=-1, keepdims=True)
        wt = jnp.where(allowed, jnp.exp(sc - top), 0.0)
        tot = jnp.sum(wt, axis=-1, keepdims=True)
        tot = jnp.where(is_live, tot, 1.0)
        prob = (wt * (1.0 / tot)).reshape(NH * 128, 128)
        low = prob.astype(BF16)
        att = dot(low, val, ((1,), (0,))).astype(BF16)
        rdot = jnp.sum(gs.astype(F32) * att.astype(F32), axis=-1, keepdims=True)
        pgrad = dot(gs, val, ((1,), (1,)))
        sg = (prob * (pgrad - rdot) * factor).astype(BF16)
        qgr = dot(sg, key, ((1,), (0,))).astype(BF16)
        for n in range(NH):
            qg[rows, HD * n:HD * n + HD] = qgr[128 * n:128 * n + 128, :]
        kvg[j, rows, :HD] = dot(sg, qs, ((0,), (0,))).astype(BF16)
        kvg[j, rows, HD:] = dot(low, gs, ((0,), (0,))).astype(BF16)
        grad_copy(j, b, kz_sem, pair_same).start()
        spread(0, b)
        grad_copy(j, b, kp_sem, partner).start()

        @pl.when(b >= 1)
        def _():
            pass_z(b - 1)
            collect(0, b - 1)

    looped(lambda b: grad_copy(j, b, kz_sem, pair_same))
    looped(lambda b: grad_copy(j, b, kp_sem, partner))
    looped(lambda b: grad_copy(tf, b, kf_sem, partner))
    for h in range(2):
        for slot in range(2):
            looped(lambda b, h=h, slot=slot: near(h, slot, b))
        looped(lambda b, h=h: far_on(h, b))
        for slot in range(3):
            looped(lambda b, h=h, slot=slot: share(h, slot, b, c))
    pass_z(NB - 1)
    collect(0, NB - 1)

    def each_block(f):
        @pl.loop(0, NB)
        def _(b):
            f(b)

    groups = (2 * zl, 2 * zl + 1, fz, fz + 1)

    def product(lhs, rhs):
        return dot(lhs.reshape(ROWS, ROWS), rhs, ((1,), (0,)))

    def own_part(h):
        mine = block_rows(h, 0)[...]
        for g in range(2):
            acc[2 * h + g] = product(mine, kvg[groups[2 * h + g]])

    def near_part(h):
        @pl.loop(0, NB)
        def _(b):
            share(h, 0, b, 1 - c).wait_recv()
            share(h, 1, b, 1 - c).wait_recv()

        for slot in range(2):
            lhs = hx[h, slot]
            for g in range(2):
                acc[2 * h + g] += product(lhs, kx[h, slot, g])

    p2 = {}

    def chunk(i, k):
        return acc[i, pl.ds(pl.multiple_of(128 * k, 128), 128), :]

    def far_part(h):
        @pl.loop(0, NB)
        def _(b):
            share(h, 2, b, 1 - c).wait_recv()

        lhs = hx[h, 2]
        o = 1 - h
        k2, kr, kl = (me[o] + 2) % 4, (me[o] + 1) % 4, (me[o] + 3) % 4
        for g in range(2):
            i = 2 * h + g
            acc[i] += product(lhs, kx[h, 2, g])
            cps = []
            for ref, src, dst, to in (
                (s_far, k2, q_far, across[o]), (s_rt, kr, q_nbl, right[o]), (s_lt, kl, q_nbr, left[o]),
            ):
                ref[i] = chunk(i, src).astype(BF16)
                cp = rcopy(ref.at[i], dst.at[i], new_sem(), to)
                cp.start()
                cps.append(cp)
            p2[i] = cps

    fin_send = new_sem(4)
    fin_recv = new_sem(4)

    def fin_copy(i, source, to):
        return pltpu.make_async_remote_copy(
            src_ref=z_acc.at[i], dst_ref=r_fin.at[source],
            send_sem=snd.at[fin_send + i], recv_sem=rcv.at[fin_recv + source],
            device_id=to, device_id_type=MESH,
        )

    def p3_start(i):
        t = groups[i]
        for cp in p2[i]:
            cp.wait_recv()
        near_sum = q_nbl[i].astype(F32) + q_nbr[i].astype(F32)
        z_acc[i] = (chunk(i, me[1 - i // 2]) + q_far[i].astype(F32)) + near_sum
        local = (zh == j) & (j == t)
        cp = fin_copy(i, zh, dev(j, y, x, t))

        @pl.when(local)
        def _():
            r_fin[zh] = z_acc[i]

        @pl.when(jnp.logical_not(local))
        def _():
            cp.start()

        @sent.append
        def _():
            @pl.when(jnp.logical_not(local))
            def _():
                cp.wait_send()

    def hidden_grad(first, last):
        @pl.loop(first, last)
        def _(n):
            cols = pl.ds(pl.multiple_of(n * 256, 256), 256)
            total = jnp.zeros((ROWS, 256), F32)
            for t in range(4):
                part = dot(kvg[t], wts[t, cols, :], ((1,), (1,)))
                total = total + part.astype(BF16).astype(F32)
            hg[:, cols] = total.astype(BF16)

    each_block(lambda b: grad_copy(pj, b, kp_sem, partner).wait_recv())
    own_part(0)
    each_block(lambda b: collect(1, b))
    for cp in h_near + h_far:
        cp.wait_recv()
    near_part(0)
    far_part(0)
    each_block(lambda b: grad_copy(tp, b, kf_sem, partner).wait_recv())
    own_part(1)
    near_part(1)
    far_part(1)
    p3_start(0)
    p3_start(1)
    p3_start(2)
    p3_start(3)
    hidden_grad(0, 8)
    for k in range(4):
        @pl.when(jnp.logical_not((zh == j) & (zh == k)))
        def _():
            fin_copy(k, k, dev(k, y, x, zh)).wait_recv()

    wg_out[...] = (r_fin[0] + r_fin[1]) + (r_fin[2] + r_fin[3])
    finish()


N_SEM = 192
N_LOC = 8


def leave(qg, hg, wg, qg_out, hg_out, wg_out, sems):
    cps = [
        pltpu.make_async_copy(src, dst, sems.at[n])
        for n, (src, dst) in enumerate(((hg, hg_out), (qg, qg_out), (wg, wg_out)))
    ]
    for cp in cps:
        cp.start()
    for cp in cps:
        cp.wait()


def on_device(hidden, kv_weight, queries, out_grad, live_blocks, doc_start):
    any_ = pl.BlockSpec(memory_space=pl.ANY)
    vmem = pl.BlockSpec(memory_space=pltpu.VMEM)
    vm = pltpu.VMEM
    results = ((ROWS, NH * HD), BF16), ((ROWS, KD), BF16), ((128, KC), F32)
    fused = pl.pallas_call(
        kernel,
        out_shape=tuple(vm(*r) for r in results),
        in_specs=[pl.BlockSpec(memory_space=pltpu.SMEM), vmem, any_, any_, any_, any_],
        out_specs=(vmem, vmem, vmem),
        scratch_shapes=[
            vm((ROWS, KD), BF16), vm((4, 4, 128, ROWS), BF16), vm((4, KD, KC), BF16),
            vm((ROWS, NH * HD), BF16), vm((ROWS, NH * HD), BF16),
            vm((ROWS, KC), F32), vm((ROWS, KC), F32), vm((ROWS, KC), F32), vm((ROWS, KC), F32),
            vm((ROWS, KC), F32), vm((ROWS, KC), F32), vm((ROWS, KC), F32),
            vm((4, ROWS, KC), BF16),
            vm((2, 3, 4, 128, ROWS), BF16),
            vm((2, 3, 2, ROWS, KC), BF16), vm((4, ROWS, KC), F32),
            vm((4, 128, KC), BF16), vm((4, 128, KC), BF16), vm((4, 128, KC), BF16),
            vm((4, 128, KC), BF16), vm((4, 128, KC), BF16), vm((4, 128, KC), BF16),
            vm((4, 128, KC), F32), vm((4, 128, KC), F32),
            pltpu.SemaphoreType.DMA((N_LOC,)),
            pltpu.SemaphoreType.DMA((N_SEM,)),
            pltpu.SemaphoreType.DMA((N_SEM,)),
        ],
        compiler_params=pltpu.CompilerParams(
            collective_id=0, has_side_effects=True, vmem_limit_bytes=58 * 1024 * 1024
        ),
        name="fused_step",
    )(live_blocks, doc_start.reshape(NB, 128), hidden, kv_weight, queries, out_grad)
    return pl.pallas_call(
        leave,
        out_shape=tuple(jax.ShapeDtypeStruct(*r) for r in results),
        in_specs=[vmem, vmem, vmem],
        out_specs=(any_, any_, any_),
        scratch_shapes=[pltpu.SemaphoreType.DMA((3,))],
        compiler_params=pltpu.CompilerParams(vmem_limit_bytes=1024 * 1024),
        name="leave",
    )(*fused)


def solution(mesh):
    in_specs = (
        P("dp", "tensor"),
        P(None, "tensor"),
        P("dp", "tensor"),
        P("dp", "tensor"),
        P("dp"),
        P("dp"),
    )
    out_specs = (P("dp", "tensor"), P("dp", "tensor"), P("dp", "tensor"))
    return jax.shard_map(
        on_device, mesh=mesh, in_specs=in_specs, out_specs=out_specs, check_vma=False
    )
```

```python
import jax
import jax.numpy as jnp
from jax import lax
from jax.experimental import pallas as pl
from jax.experimental.pallas import tpu as pltpu
from jax.sharding import PartitionSpec as P

BF16 = jnp.bfloat16
F32 = jnp.float32
I16 = jnp.int16
HD = 128
ROWS = 512
NB = 4
NH = 8
KD = 2048
KC = 256
MESH = pl.DeviceIdType.MESH


def dot(a, b, dims):
    return lax.dot_general(a, b, (dims, ((), ())), preferred_element_type=F32)


def code(v):
    top = jnp.max(jnp.abs(v), axis=0, keepdims=True)
    inv = jnp.where(top > 0.0, 1.0 / top, 0.0)
    n = v * inv * 32767.0
    n = n + jnp.where(n >= 0.0, 0.5, -0.5)
    return n.astype(jnp.int32).astype(jnp.int16), jnp.broadcast_to(top, (8, KC))


def decode(n, top):
    return n.astype(jnp.int32).astype(F32) * (1.0 / 32767.0) * top[0:1, :]


def kernel(
    live_ref, start_ref, hid_hbm, w_hbm, q_hbm, g_hbm,
    qg, hg, wg_out,
    hid, hid_t, wts, qv, gv,
    own, pp, pf, ff, r_pp, r_pf, r_z, kvg,
    hx, kx, acc, s_far, s_rt, s_lt, q_far, q_nbl, q_nbr, s_t, q_t,
    z_q, z_t, r_fin, r_ft,
    loc, snd, rcv,
):
    counter = [0, 0]

    def new_sem(count=1):
        first = counter[0]
        counter[0] += count
        return first

    def new_loc():
        counter[1] += 1
        return loc.at[counter[1] - 1]

    dp = lax.axis_index("dp")
    j = lax.axis_index("tensor")
    zh = dp // 16
    y = (dp // 4) % 4
    x = dp % 4
    zl = j // 2
    c = j % 2
    pj = 2 * zl + 1 - c
    fz = 2 * (1 - zl)
    tf = fz + c
    tp = fz + 1 - c

    def dev(zh_, y_, x_, t_):
        return {"dp": zh_ * 16 + y_ * 4 + x_, "tensor": t_}

    partner = dev(zh, y, x, pj)
    pair_same = dev(zh, y, x, tf)
    pair_other = dev(zh, y, x, tp)
    zo = (zh + 2 * zl + 3) % 4
    oth_same = dev(zo, y, x, tf)
    oth_other = dev(zo, y, x, tp)
    right = (dev(zh, y, (x + 1) % 4, j), dev(zh, (y + 1) % 4, x, j))
    left = (dev(zh, y, (x + 3) % 4, j), dev(zh, (y + 3) % 4, x, j))
    across = (dev(zh, y, (x + 2) % 4, j), dev(zh, (y + 2) % 4, x, j))
    me = (x, y)

    sent = []

    def finish():
        for wait in sent:
            wait()

    def rcopy(src, dst, sem, to, keep=True):
        cp = pltpu.make_async_remote_copy(
            src_ref=src, dst_ref=dst, send_sem=snd.at[sem], recv_sem=rcv.at[sem],
            device_id=to, device_id_type=MESH,
        )
        if keep:
            sent.append(cp.wait_send)
        return cp

    def looped(make):
        def wait():
            @pl.loop(0, NB)
            def _(b):
                make(b).wait_send()

        sent.append(wait)

    cp_own = pltpu.make_async_copy(w_hbm.at[pl.ds(KD * j, KD), :], wts.at[j], new_loc())
    cp_own.start()
    cp_hid = pltpu.make_async_copy(hid_hbm, hid, new_loc())
    cp_hid.start()

    barrier = pltpu.get_barrier_semaphore()

    def greet(to):
        pl.semaphore_signal(barrier, inc=1, device_id=to, device_id_type=MESH)

    for to in (partner, pair_same, pair_other, oth_same, oth_other) + right + left + across:
        greet(to)
    for k in range(4):
        @pl.when(jnp.logical_not((zh == j) & (j == k)))
        def _():
            greet(dev(j, y, x, k))

        @pl.when(jnp.logical_not((zh == j) & (zh == k)))
        def _():
            greet(dev(k, y, x, zh))
    own_case = jnp.where(zh == j, 1, 0)
    pl.semaphore_wait(barrier, 19 - 2 * own_case)

    order = (0, 2, 1, 3)

    def piece_row(h, n):
        return 1024 * h + 512 * (me[h] % 2) + 128 * n

    cp_z = {}
    for k in range(2):
        cd = (1 - c) if k == 0 else c
        td = fz + cd
        for n in order:
            for h in range(2):
                to = ((pair_other, pair_same), (oth_other, oth_same))[h][k]
                off = piece_row(h, n)
                cp = rcopy(
                    w_hbm.at[pl.ds(KD * td + off, 128), :],
                    wts.at[j, pl.ds(off, 128), :], new_sem(), to,
                )
                cp.start()
                cp_z[k, n, h] = cp
    cp_pw = rcopy(w_hbm.at[pl.ds(KD * pj, KD), :], wts.at[j], new_sem(), partner)
    cp_pw.start()
    cp_q = pltpu.make_async_copy(q_hbm, qv, new_loc())
    cp_q.start()
    cp_g = pltpu.make_async_copy(g_hbm, gv, new_loc())
    cp_g.start()

    def proj(t, store):
        @pl.loop(0, 2)
        def _(n):
            rows = pl.ds(n * 256, 256)
            store(rows, dot(hid[rows, :], wts[t], ((1,), (0,))))

    def to_ref(ref):
        def store(rows, value):
            ref[rows, :] = value
        return store

    far = {0: [], 1: []}

    def ring(k):
        for n in order:
            for h in range(2):
                cp_z[k, n, h].wait_recv()
                ref = wts.at[(tp, tf)[k], pl.ds(piece_row(h, n), 128), :]
                cp = rcopy(ref, ref, new_sem(), right[h] if n < 2 else left[h])
                cp.start()
                far[k].append(cp)

    cp_hid.wait()

    @pl.loop(0, 4)
    def _(k):
        for n in range(4):
            cols = pl.ds(pl.multiple_of(512 * k + 128 * n, 128), 128)
            hid_t[k, n] = hid[:, cols].T

    def block_rows(h, step):
        dest = (me[h] + step) % 4
        return hid_t.at[:, dest] if h == 0 else hid_t.at[dest]

    h_near, h_far = [], []

    def send_hidden(first, size):
        for h in range(2):
            for slot, step, to in ((0, 1, right[h]), (1, 3, left[h])):
                part = pl.ds(first, size)
                cp = rcopy(block_rows(h, step).at[part], hx.at[h, slot, part], new_sem(), to)
                cp.start()
                h_near.append(cp)

    def send_hidden_rest():
        send_hidden(2, 2)
        for h in range(2):
            cp = rcopy(block_rows(h, 2), hx.at[h, 2], new_sem(), across[h])
            cp.start()
            h_far.append(cp)

    send_hidden(0, 2)
    ring(0)
    cp_own.wait()
    proj(j, to_ref(own))
    ring(1)
    cp_pw.wait_recv()
    proj(pj, to_ref(pp))
    cp_pp = rcopy(pp, r_pp, new_sem(), partner)
    cp_pp.start()

    send_hidden_rest()

    for cp in far[0]:
        cp.wait_recv()
    proj(tp, to_ref(pf))
    cp_pf = rcopy(pf, r_pf, new_sem(), partner)
    cp_pf.start()
    for cp in far[1]:
        cp.wait_recv()
    proj(tf, to_ref(ff))
    cp_pf.wait_recv()
    z_sem = new_sem(NB)

    def block_z(b):
        rows = pl.ds(b * 128, 128)
        return rcopy(ff.at[rows, :], r_z.at[rows, :], z_sem + b, pair_same, keep=False)

    @pl.loop(0, NB)
    def _(b):
        rows = pl.ds(b * 128, 128)
        ff[rows, :] = ff[rows, :] + r_pf[rows, :]
        block_z(b).start()

    looped(block_z)
    cp_pp.wait_recv()
    cp_q.wait()
    cp_g.wait()
    live = live_ref[0]
    factor = HD ** -0.5
    kp_sem = new_sem(NB)
    kz_sem = new_sem(NB)
    kf_sem = new_sem(NB)

    def grad_copy(t, b, sem, to):
        ref = kvg.at[t, pl.ds(b * 128, 128), :]
        return rcopy(ref, ref, sem + b, to, keep=False)

    near_sem = [[new_sem(NB), new_sem(NB)] for _ in range(2)]
    far_sem = [new_sem(NB) for _ in range(2)]
    share_sem = [[new_sem(NB) for _ in range(3)] for _ in range(2)]
    group = (j, tf)

    def near(h, slot, b):
        rows = pl.ds(b * 128, 128)
        return rcopy(
            kvg.at[group[h], rows, :], kx.at[h, slot, c, rows, :], near_sem[h][slot] + b,
            (right, left)[slot][h], keep=False,
        )

    def far_on(h, b):
        rows = pl.ds(b * 128, 128)
        return rcopy(
            kvg.at[group[h], rows, :], kx.at[h, 2, c, rows, :], far_sem[h] + b,
            across[h], keep=False,
        )

    def spread(h, b):
        near(h, 0, b).start()
        near(h, 1, b).start()
        far_on(h, b).start()

    def share(h, slot, b, g):
        ref = kx.at[h, slot, g, pl.ds(b * 128, 128), :]
        return rcopy(ref, ref, share_sem[h][slot] + b, partner, keep=False)

    def collect(h, b):
        near(h, 0, b).wait_recv()
        share(h, 0, b, c).start()
        near(h, 1, b).wait_recv()
        share(h, 1, b, c).start()
        far_on(h, b).wait_recv()
        share(h, 2, b, c).start()

    def pass_z(b):
        grad_copy(tf, b, kz_sem, pair_same).wait_recv()
        spread(1, b)
        grad_copy(tf, b, kf_sem, partner).start()

    @pl.loop(0, NB)
    def _(b):
        rows = pl.ds(b * 128, 128)
        block_z(b).wait_recv()
        kv = (own[rows, :] + r_pp[rows, :] + r_z[rows, :]).astype(BF16)
        key, val = kv[:, :HD], kv[:, HD:]
        qs = jnp.concatenate([qv[rows, HD * n:HD * n + HD] for n in range(NH)], axis=0)
        gs = jnp.concatenate([gv[rows, HD * n:HD * n + HD] for n in range(NH)], axis=0)
        start = jnp.broadcast_to(start_ref[pl.ds(b, 1), :], (128, 128)).T
        pos_u = lax.broadcasted_iota(jnp.int32, (128, 128), 1)
        pos_t = lax.broadcasted_iota(jnp.int32, (128, 128), 0)
        is_live = b < live
        lim = jnp.where(is_live, pos_t, -1)
        allowed = ((pos_u >= start) & (pos_u <= lim))[None]
        sc = (dot(qs, key, ((1,), (1,))) * factor).reshape(NH, 128, 128)
        top = jnp.max(jnp.where(allowed, sc, -1e30), axis=-1, keepdims=True)
        wt = jnp.where(allowed, jnp.exp(sc - top), 0.0)
        tot = jnp.sum(wt, axis=-1, keepdims=True)
        tot = jnp.where(is_live, tot, 1.0)
        prob = (wt * (1.0 / tot)).reshape(NH * 128, 128)
        low = prob.astype(BF16)
        att = dot(low, val, ((1,), (0,))).astype(BF16)
        rdot = jnp.sum(gs.astype(F32) * att.astype(F32), axis=-1, keepdims=True)
        pgrad = dot(gs, val, ((1,), (1,)))
        sg = (prob * (pgrad - rdot) * factor).astype(BF16)
        qgr = dot(sg, key, ((1,), (0,))).astype(BF16)
        for n in range(NH):
            qg[rows, HD * n:HD * n + HD] = qgr[128 * n:128 * n + 128, :]
        kvg[j, rows, :HD] = dot(sg, qs, ((0,), (0,))).astype(BF16)
        kvg[j, rows, HD:] = dot(low, gs, ((0,), (0,))).astype(BF16)
        grad_copy(j, b, kz_sem, pair_same).start()
        spread(0, b)
        grad_copy(j, b, kp_sem, partner).start()

        @pl.when(b >= 1)
        def _():
            pass_z(b - 1)
            collect(0, b - 1)

    looped(lambda b: grad_copy(j, b, kz_sem, pair_same))
    looped(lambda b: grad_copy(j, b, kp_sem, partner))
    looped(lambda b: grad_copy(tf, b, kf_sem, partner))
    for h in range(2):
        for slot in range(2):
            looped(lambda b, h=h, slot=slot: near(h, slot, b))
        looped(lambda b, h=h: far_on(h, b))
        for slot in range(3):
            looped(lambda b, h=h, slot=slot: share(h, slot, b, c))
    pass_z(NB - 1)
    collect(0, NB - 1)

    def each_block(f):
        @pl.loop(0, NB)
        def _(b):
            f(b)

    groups = (2 * zl, 2 * zl + 1, fz, fz + 1)

    def product(lhs, rhs):
        return dot(lhs.reshape(ROWS, ROWS), rhs, ((1,), (0,)))

    def own_part(h):
        mine = block_rows(h, 0)[...]
        for g in range(2):
            acc[2 * h + g] = product(mine, kvg[groups[2 * h + g]])

    def near_part(h):
        @pl.loop(0, NB)
        def _(b):
            share(h, 0, b, 1 - c).wait_recv()
            share(h, 1, b, 1 - c).wait_recv()

        for slot in range(2):
            lhs = hx[h, slot]
            for g in range(2):
                acc[2 * h + g] += product(lhs, kx[h, slot, g])

    p2 = {}

    def chunk(i, k):
        return acc[i, pl.ds(pl.multiple_of(128 * k, 128), 128), :]

    def far_part(h):
        @pl.loop(0, NB)
        def _(b):
            share(h, 2, b, 1 - c).wait_recv()

        lhs = hx[h, 2]
        o = 1 - h
        k2, kr, kl = (me[o] + 2) % 4, (me[o] + 1) % 4, (me[o] + 3) % 4
        for g in range(2):
            i = 2 * h + g
            acc[i] += product(lhs, kx[h, 2, g])
            cps = []
            for n, (ref, src, dst, to) in enumerate((
                (s_far, k2, q_far, across[o]), (s_rt, kr, q_nbl, right[o]), (s_lt, kl, q_nbr, left[o]),
            )):
                ref[i], s_t[n, i] = code(chunk(i, src))
                for a, b in ((s_t.at[n, i], q_t.at[n, i]), (ref.at[i], dst.at[i])):
                    cp = rcopy(a, b, new_sem(), to)
                    cp.start()
                    cps.append(cp)
            p2[i] = cps

    fin_send = new_sem(8)
    fin_recv = new_sem(8)

    def fin_copies(i, source, to):
        return [
            pltpu.make_async_remote_copy(
                src_ref=src.at[i], dst_ref=dst.at[source],
                send_sem=snd.at[fin_send + 4 * n + i], recv_sem=rcv.at[fin_recv + 4 * n + source],
                device_id=to, device_id_type=MESH,
            )
            for n, (src, dst) in enumerate(((z_t, r_ft), (z_q, r_fin)))
        ]

    def p3_start(i):
        t = groups[i]
        for cp in p2[i]:
            cp.wait_recv()
        near_sum = decode(q_nbl[i], q_t[1, i]) + decode(q_nbr[i], q_t[2, i])
        z_q[i], z_t[i] = code((chunk(i, me[1 - i // 2]) + decode(q_far[i], q_t[0, i])) + near_sum)
        local = (zh == j) & (j == t)
        cps = fin_copies(i, zh, dev(j, y, x, t))

        @pl.when(local)
        def _():
            r_fin[zh] = z_q[i]
            r_ft[zh] = z_t[i]

        @pl.when(jnp.logical_not(local))
        def _():
            for cp in cps:
                cp.start()

        @sent.append
        def _():
            @pl.when(jnp.logical_not(local))
            def _():
                for cp in cps:
                    cp.wait_send()

    def hidden_grad(first, last):
        @pl.loop(first, last)
        def _(n):
            cols = pl.ds(pl.multiple_of(n * 256, 256), 256)
            total = jnp.zeros((ROWS, 256), F32)
            for t in range(4):
                part = dot(kvg[t], wts[t, cols, :], ((1,), (1,)))
                total = total + part.astype(BF16).astype(F32)
            hg[:, cols] = total.astype(BF16)

    each_block(lambda b: grad_copy(pj, b, kp_sem, partner).wait_recv())
    own_part(0)
    each_block(lambda b: collect(1, b))
    for cp in h_near + h_far:
        cp.wait_recv()
    near_part(0)
    far_part(0)
    each_block(lambda b: grad_copy(tp, b, kf_sem, partner).wait_recv())
    own_part(1)
    near_part(1)
    far_part(1)
    p3_start(0)
    p3_start(1)
    hidden_grad(0, 1)
    p3_start(2)
    p3_start(3)
    hidden_grad(1, 8)
    for k in range(4):
        @pl.when(jnp.logical_not((zh == j) & (zh == k)))
        def _():
            for cp in fin_copies(k, k, dev(k, y, x, zh)):
                cp.wait_recv()

    parts = [decode(r_fin[k], r_ft[k]) for k in range(4)]
    wg_out[...] = (parts[0] + parts[1]) + (parts[2] + parts[3])
    finish()


N_SEM = 192
N_LOC = 8


def leave(qg, hg, wg, qg_out, hg_out, wg_out, sems):
    cps = [
        pltpu.make_async_copy(src, dst, sems.at[n])
        for n, (src, dst) in enumerate(((hg, hg_out), (qg, qg_out), (wg, wg_out)))
    ]
    for cp in cps:
        cp.start()
    for cp in cps:
        cp.wait()


def on_device(hidden, kv_weight, queries, out_grad, live_blocks, doc_start):
    any_ = pl.BlockSpec(memory_space=pl.ANY)
    vmem = pl.BlockSpec(memory_space=pltpu.VMEM)
    vm = pltpu.VMEM
    results = ((ROWS, NH * HD), BF16), ((ROWS, KD), BF16), ((128, KC), F32)
    fused = pl.pallas_call(
        kernel,
        out_shape=tuple(vm(*r) for r in results),
        in_specs=[pl.BlockSpec(memory_space=pltpu.SMEM), vmem, any_, any_, any_, any_],
        out_specs=(vmem, vmem, vmem),
        scratch_shapes=[
            vm((ROWS, KD), BF16), vm((4, 4, 128, ROWS), BF16), vm((4, KD, KC), BF16),
            vm((ROWS, NH * HD), BF16), vm((ROWS, NH * HD), BF16),
            vm((ROWS, KC), F32), vm((ROWS, KC), F32), vm((ROWS, KC), F32), vm((ROWS, KC), F32),
            vm((ROWS, KC), F32), vm((ROWS, KC), F32), vm((ROWS, KC), F32),
            vm((4, ROWS, KC), BF16),
            vm((2, 3, 4, 128, ROWS), BF16),
            vm((2, 3, 2, ROWS, KC), BF16), vm((4, ROWS, KC), F32),
            vm((4, 128, KC), I16), vm((4, 128, KC), I16), vm((4, 128, KC), I16),
            vm((4, 128, KC), I16), vm((4, 128, KC), I16), vm((4, 128, KC), I16),
            vm((3, 4, 8, KC), F32), vm((3, 4, 8, KC), F32),
            vm((4, 128, KC), I16), vm((4, 8, KC), F32), vm((4, 128, KC), I16), vm((4, 8, KC), F32),
            pltpu.SemaphoreType.DMA((N_LOC,)),
            pltpu.SemaphoreType.DMA((N_SEM,)),
            pltpu.SemaphoreType.DMA((N_SEM,)),
        ],
        compiler_params=pltpu.CompilerParams(
            collective_id=0, has_side_effects=True, vmem_limit_bytes=58 * 1024 * 1024
        ),
        name="fused_step",
    )(live_blocks, doc_start.reshape(NB, 128), hidden, kv_weight, queries, out_grad)
    return pl.pallas_call(
        leave,
        out_shape=tuple(jax.ShapeDtypeStruct(*r) for r in results),
        in_specs=[vmem, vmem, vmem],
        out_specs=(any_, any_, any_),
        scratch_shapes=[pltpu.SemaphoreType.DMA((3,))],
        compiler_params=pltpu.CompilerParams(vmem_limit_bytes=1024 * 1024),
        name="leave",
    )(*fused)


def solution(mesh):
    in_specs = (
        P("dp", "tensor"),
        P(None, "tensor"),
        P("dp", "tensor"),
        P("dp", "tensor"),
        P("dp"),
        P("dp"),
    )
    out_specs = (P("dp", "tensor"), P("dp", "tensor"), P("dp", "tensor"))
    return jax.shard_map(
        on_device, mesh=mesh, in_specs=in_specs, out_specs=out_specs, check_vma=False
    )
```

```python
import jax
import jax.numpy as jnp
from jax import lax
from jax.experimental import pallas as pl
from jax.experimental.pallas import tpu as pltpu
from jax.sharding import PartitionSpec as P

BF16 = jnp.bfloat16
F32 = jnp.float32
I16 = jnp.int16
HD = 128
ROWS = 512
NB = 4
NH = 8
KD = 2048
KC = 256
MESH = pl.DeviceIdType.MESH


def dot(a, b, dims):
    return lax.dot_general(a, b, (dims, ((), ())), preferred_element_type=F32)


def code(v):
    top = jnp.max(jnp.abs(v), axis=0, keepdims=True)
    inv = jnp.where(top > 0.0, 1.0 / top, 0.0)
    n = v * inv * 32767.0
    n = n + jnp.where(n >= 0.0, 0.5, -0.5)
    return n.astype(jnp.int32).astype(jnp.int16), jnp.broadcast_to(top, (8, KC))


def decode(n, top):
    return n.astype(jnp.int32).astype(F32) * (1.0 / 32767.0) * top[0:1, :]


def kernel(
    live_ref, start_ref, hid_hbm, w_hbm, q_hbm, g_hbm,
    qg, hg, wg_out,
    hid, hid_t, wts, qv, gv,
    own, pp, pf, ff, r_pp, r_pf, r_z, kvg,
    hx, kx, acc, s_far, s_rt, s_lt, q_far, q_nbl, q_nbr, s_t, q_t,
    z_q, z_t, r_fin, r_ft,
    loc, snd, rcv,
):
    counter = [0, 0]

    def new_sem(count=1):
        first = counter[0]
        counter[0] += count
        return first

    def new_loc():
        counter[1] += 1
        return loc.at[counter[1] - 1]

    dp = lax.axis_index("dp")
    j = lax.axis_index("tensor")
    zh = dp // 16
    y = (dp // 4) % 4
    x = dp % 4
    zl = j // 2
    c = j % 2
    pj = 2 * zl + 1 - c
    fz = 2 * (1 - zl)
    tf = fz + c
    tp = fz + 1 - c

    def dev(zh_, y_, x_, t_):
        return {"dp": zh_ * 16 + y_ * 4 + x_, "tensor": t_}

    partner = dev(zh, y, x, pj)
    pair_same = dev(zh, y, x, tf)
    pair_other = dev(zh, y, x, tp)
    zo = (zh + 2 * zl + 3) % 4
    oth_same = dev(zo, y, x, tf)
    oth_other = dev(zo, y, x, tp)
    right = (dev(zh, y, (x + 1) % 4, j), dev(zh, (y + 1) % 4, x, j))
    left = (dev(zh, y, (x + 3) % 4, j), dev(zh, (y + 3) % 4, x, j))
    across = (dev(zh, y, (x + 2) % 4, j), dev(zh, (y + 2) % 4, x, j))
    me = (x, y)

    sent = []

    def finish():
        for wait in sent:
            wait()

    def rcopy(src, dst, sem, to, keep=True):
        cp = pltpu.make_async_remote_copy(
            src_ref=src, dst_ref=dst, send_sem=snd.at[sem], recv_sem=rcv.at[sem],
            device_id=to, device_id_type=MESH,
        )
        if keep:
            sent.append(cp.wait_send)
        return cp

    def looped(make):
        def wait():
            @pl.loop(0, NB)
            def _(b):
                make(b).wait_send()

        sent.append(wait)

    cp_own = pltpu.make_async_copy(w_hbm.at[pl.ds(KD * j, KD), :], wts.at[j], new_loc())
    cp_own.start()
    cp_hid = pltpu.make_async_copy(hid_hbm, hid, new_loc())
    cp_hid.start()

    barrier = pltpu.get_barrier_semaphore()

    def greet(to):
        pl.semaphore_signal(barrier, inc=1, device_id=to, device_id_type=MESH)

    for to in (partner, pair_same, pair_other, oth_same, oth_other) + right + left + across:
        greet(to)
    for k in range(4):
        @pl.when(jnp.logical_not((zh == j) & (j == k)))
        def _():
            greet(dev(j, y, x, k))

        @pl.when(jnp.logical_not((zh == j) & (zh == k)))
        def _():
            greet(dev(k, y, x, zh))
    own_case = jnp.where(zh == j, 1, 0)

    def transpose(first, last):
        @pl.loop(first, last)
        def _(k):
            for n in range(4):
                cols = pl.ds(pl.multiple_of(512 * k + 128 * n, 128), 128)
                hid_t[k, n] = hid[:, cols].T

    cp_hid.wait()
    transpose(0, 2)
    pl.semaphore_wait(barrier, 19 - 2 * own_case)

    order = (0, 2, 1, 3)

    def piece_row(h, n):
        return 1024 * h + 512 * (me[h] % 2) + 128 * n

    cp_z = {}
    for k in range(2):
        cd = (1 - c) if k == 0 else c
        td = fz + cd
        for n in order:
            for h in range(2):
                to = ((pair_other, pair_same), (oth_other, oth_same))[h][k]
                off = piece_row(h, n)
                cp = rcopy(
                    w_hbm.at[pl.ds(KD * td + off, 128), :],
                    wts.at[j, pl.ds(off, 128), :], new_sem(), to,
                )
                cp.start()
                cp_z[k, n, h] = cp
    cp_pw = rcopy(w_hbm.at[pl.ds(KD * pj, KD), :], wts.at[j], new_sem(), partner)
    cp_pw.start()
    cp_q = pltpu.make_async_copy(q_hbm, qv, new_loc())
    cp_q.start()
    cp_g = pltpu.make_async_copy(g_hbm, gv, new_loc())
    cp_g.start()

    def proj(t, store):
        @pl.loop(0, 2)
        def _(n):
            rows = pl.ds(n * 256, 256)
            store(rows, dot(hid[rows, :], wts[t], ((1,), (0,))))

    def to_ref(ref):
        def store(rows, value):
            ref[rows, :] = value
        return store

    far = {0: [], 1: []}

    def ring(k):
        for n in order:
            for h in range(2):
                cp_z[k, n, h].wait_recv()
                ref = wts.at[(tp, tf)[k], pl.ds(piece_row(h, n), 128), :]
                cp = rcopy(ref, ref, new_sem(), right[h] if n < 2 else left[h])
                cp.start()
                far[k].append(cp)

    transpose(2, 4)

    def block_rows(h, step):
        dest = (me[h] + step) % 4
        return hid_t.at[:, dest] if h == 0 else hid_t.at[dest]

    h_near, h_far = [], []

    def send_hidden(first, size):
        for h in range(2):
            for slot, step, to in ((0, 1, right[h]), (1, 3, left[h])):
                part = pl.ds(first, size)
                cp = rcopy(block_rows(h, step).at[part], hx.at[h, slot, part], new_sem(), to)
                cp.start()
                h_near.append(cp)

    def send_hidden_rest():
        send_hidden(2, 2)
        for h in range(2):
            cp = rcopy(block_rows(h, 2), hx.at[h, 2], new_sem(), across[h])
            cp.start()
            h_far.append(cp)

    send_hidden(0, 2)
    ring(0)
    cp_own.wait()
    proj(j, to_ref(own))
    ring(1)
    send_hidden_rest()
    cp_pw.wait_recv()
    proj(pj, to_ref(pp))
    cp_pp = rcopy(pp, r_pp, new_sem(), partner)
    cp_pp.start()

    for cp in far[0]:
        cp.wait_recv()
    proj(tp, to_ref(pf))
    cp_pf = rcopy(pf, r_pf, new_sem(), partner)
    cp_pf.start()
    for cp in far[1]:
        cp.wait_recv()
    proj(tf, to_ref(ff))
    cp_pf.wait_recv()
    z_sem = new_sem(NB)

    def block_z(b):
        rows = pl.ds(b * 128, 128)
        return rcopy(ff.at[rows, :], r_z.at[rows, :], z_sem + b, pair_same, keep=False)

    @pl.loop(0, NB)
    def _(b):
        rows = pl.ds(b * 128, 128)
        ff[rows, :] = ff[rows, :] + r_pf[rows, :]
        block_z(b).start()

    looped(block_z)
    cp_pp.wait_recv()
    cp_q.wait()
    cp_g.wait()
    live = live_ref[0]
    factor = HD ** -0.5
    kp_sem = new_sem(NB)
    kz_sem = new_sem(NB)
    kf_sem = new_sem(NB)

    def grad_copy(t, b, sem, to):
        ref = kvg.at[t, pl.ds(b * 128, 128), :]
        return rcopy(ref, ref, sem + b, to, keep=False)

    near_sem = [[new_sem(NB), new_sem(NB)] for _ in range(2)]
    far_sem = [new_sem(NB) for _ in range(2)]
    share_sem = [[new_sem(NB) for _ in range(3)] for _ in range(2)]
    group = (j, tf)

    def near(h, slot, b):
        rows = pl.ds(b * 128, 128)
        return rcopy(
            kvg.at[group[h], rows, :], kx.at[h, slot, c, rows, :], near_sem[h][slot] + b,
            (right, left)[slot][h], keep=False,
        )

    def far_on(h, b):
        rows = pl.ds(b * 128, 128)
        return rcopy(
            kvg.at[group[h], rows, :], kx.at[h, 2, c, rows, :], far_sem[h] + b,
            across[h], keep=False,
        )

    def spread(h, b):
        near(h, 0, b).start()
        near(h, 1, b).start()
        far_on(h, b).start()

    def share(h, slot, b, g):
        ref = kx.at[h, slot, g, pl.ds(b * 128, 128), :]
        return rcopy(ref, ref, share_sem[h][slot] + b, partner, keep=False)

    def collect(h, b):
        near(h, 0, b).wait_recv()
        share(h, 0, b, c).start()
        near(h, 1, b).wait_recv()
        share(h, 1, b, c).start()
        far_on(h, b).wait_recv()
        share(h, 2, b, c).start()

    def pass_z(b):
        grad_copy(tf, b, kz_sem, pair_same).wait_recv()
        spread(1, b)
        grad_copy(tf, b, kf_sem, partner).start()

    @pl.loop(0, NB)
    def _(b):
        rows = pl.ds(b * 128, 128)
        block_z(b).wait_recv()
        kv = (own[rows, :] + r_pp[rows, :] + r_z[rows, :]).astype(BF16)
        key, val = kv[:, :HD], kv[:, HD:]
        qs = jnp.concatenate([qv[rows, HD * n:HD * n + HD] for n in range(NH)], axis=0)
        gs = jnp.concatenate([gv[rows, HD * n:HD * n + HD] for n in range(NH)], axis=0)
        start = jnp.broadcast_to(start_ref[pl.ds(b, 1), :], (128, 128)).T
        pos_u = lax.broadcasted_iota(jnp.int32, (128, 128), 1)
        pos_t = lax.broadcasted_iota(jnp.int32, (128, 128), 0)
        is_live = b < live
        lim = jnp.where(is_live, pos_t, -1)
        allowed = ((pos_u >= start) & (pos_u <= lim))[None]
        sc = (dot(qs, key, ((1,), (1,))) * factor).reshape(NH, 128, 128)
        top = jnp.max(jnp.where(allowed, sc, -1e30), axis=-1, keepdims=True)
        wt = jnp.where(allowed, jnp.exp(sc - top), 0.0)
        tot = jnp.sum(wt, axis=-1, keepdims=True)
        tot = jnp.where(is_live, tot, 1.0)
        prob = (wt * (1.0 / tot)).reshape(NH * 128, 128)
        low = prob.astype(BF16)
        att = dot(low, val, ((1,), (0,))).astype(BF16)
        rdot = jnp.sum(gs.astype(F32) * att.astype(F32), axis=-1, keepdims=True)
        pgrad = dot(gs, val, ((1,), (1,)))
        sg = (prob * (pgrad - rdot) * factor).astype(BF16)
        qgr = dot(sg, key, ((1,), (0,))).astype(BF16)
        for n in range(NH):
            qg[rows, HD * n:HD * n + HD] = qgr[128 * n:128 * n + 128, :]
        kvg[j, rows, :HD] = dot(sg, qs, ((0,), (0,))).astype(BF16)
        kvg[j, rows, HD:] = dot(low, gs, ((0,), (0,))).astype(BF16)
        grad_copy(j, b, kz_sem, pair_same).start()
        spread(0, b)
        grad_copy(j, b, kp_sem, partner).start()

        @pl.when(b >= 1)
        def _():
            pass_z(b - 1)

    looped(lambda b: grad_copy(j, b, kz_sem, pair_same))
    looped(lambda b: grad_copy(j, b, kp_sem, partner))
    looped(lambda b: grad_copy(tf, b, kf_sem, partner))
    for h in range(2):
        for slot in range(2):
            looped(lambda b, h=h, slot=slot: near(h, slot, b))
        looped(lambda b, h=h: far_on(h, b))
        for slot in range(3):
            looped(lambda b, h=h, slot=slot: share(h, slot, b, c))
    pass_z(NB - 1)

    def each_block(f):
        @pl.loop(0, NB)
        def _(b):
            f(b)

    groups = (2 * zl, 2 * zl + 1, fz, fz + 1)

    def product(lhs, rhs):
        return dot(lhs.reshape(ROWS, ROWS), rhs, ((1,), (0,)))

    def own_part(h):
        mine = block_rows(h, 0)[...]
        for g in range(2):
            acc[2 * h + g] = product(mine, kvg[groups[2 * h + g]])

    def near_part(h):
        @pl.loop(0, NB)
        def _(b):
            share(h, 0, b, 1 - c).wait_recv()
            share(h, 1, b, 1 - c).wait_recv()

        for slot in range(2):
            lhs = hx[h, slot]
            for g in range(2):
                acc[2 * h + g] += product(lhs, kx[h, slot, g])

    p2 = {}

    def chunk(i, k):
        return acc[i, pl.ds(pl.multiple_of(128 * k, 128), 128), :]

    def far_part(h):
        @pl.loop(0, NB)
        def _(b):
            share(h, 2, b, 1 - c).wait_recv()

        lhs = hx[h, 2]
        o = 1 - h
        k2, kr, kl = (me[o] + 2) % 4, (me[o] + 1) % 4, (me[o] + 3) % 4
        for g in range(2):
            i = 2 * h + g
            acc[i] += product(lhs, kx[h, 2, g])
            cps = []
            for n, (ref, src, dst, to) in enumerate((
                (s_far, k2, q_far, across[o]), (s_rt, kr, q_nbl, right[o]), (s_lt, kl, q_nbr, left[o]),
            )):
                ref[i], s_t[n, i] = code(chunk(i, src))
                for a, b in ((s_t.at[n, i], q_t.at[n, i]), (ref.at[i], dst.at[i])):
                    cp = rcopy(a, b, new_sem(), to)
                    cp.start()
                    cps.append(cp)
            p2[i] = cps

    fin_send = new_sem(8)
    fin_recv = new_sem(8)

    def fin_copies(i, source, to):
        return [
            pltpu.make_async_remote_copy(
                src_ref=src.at[i], dst_ref=dst.at[source],
                send_sem=snd.at[fin_send + 4 * n + i], recv_sem=rcv.at[fin_recv + 4 * n + source],
                device_id=to, device_id_type=MESH,
            )
            for n, (src, dst) in enumerate(((z_t, r_ft), (z_q, r_fin)))
        ]

    def p3_start(i):
        t = groups[i]
        for cp in p2[i]:
            cp.wait_recv()
        near_sum = decode(q_nbl[i], q_t[1, i]) + decode(q_nbr[i], q_t[2, i])
        z_q[i], z_t[i] = code((chunk(i, me[1 - i // 2]) + decode(q_far[i], q_t[0, i])) + near_sum)
        local = (zh == j) & (j == t)
        cps = fin_copies(i, zh, dev(j, y, x, t))

        @pl.when(local)
        def _():
            r_fin[zh] = z_q[i]
            r_ft[zh] = z_t[i]

        @pl.when(jnp.logical_not(local))
        def _():
            for cp in cps:
                cp.start()

        @sent.append
        def _():
            @pl.when(jnp.logical_not(local))
            def _():
                for cp in cps:
                    cp.wait_send()

    def hidden_grad(first, last):
        @pl.loop(first, last)
        def _(n):
            cols = pl.ds(pl.multiple_of(n * 256, 256), 256)
            total = jnp.zeros((ROWS, 256), F32)
            for t in range(4):
                part = dot(kvg[t], wts[t, cols, :], ((1,), (1,)))
                total = total + part.astype(BF16).astype(F32)
            hg[:, cols] = total.astype(BF16)

    each_block(lambda b: grad_copy(pj, b, kp_sem, partner).wait_recv())
    own_part(0)
    each_block(lambda b: collect(0, b))
    each_block(lambda b: grad_copy(tp, b, kf_sem, partner).wait_recv())
    own_part(1)

    @pl.loop(0, NB - 1)
    def _(b):
        collect(1, b)

    for cp in h_near:
        cp.wait_recv()
    near_part(0)
    collect(1, NB - 1)
    for cp in h_far:
        cp.wait_recv()
    far_part(0)
    near_part(1)
    far_part(1)
    p3_start(0)
    p3_start(1)
    hidden_grad(0, 1)
    p3_start(2)
    p3_start(3)
    hidden_grad(1, 8)
    for k in range(4):
        @pl.when(jnp.logical_not((zh == j) & (zh == k)))
        def _():
            for cp in fin_copies(k, k, dev(k, y, x, zh)):
                cp.wait_recv()

    parts = [decode(r_fin[k], r_ft[k]) for k in range(4)]
    wg_out[...] = (parts[0] + parts[1]) + (parts[2] + parts[3])
    finish()


N_SEM = 192
N_LOC = 8


def leave(qg, hg, wg, qg_out, hg_out, wg_out, sems):
    cps = [
        pltpu.make_async_copy(src, dst, sems.at[n])
        for n, (src, dst) in enumerate(((hg, hg_out), (qg, qg_out), (wg, wg_out)))
    ]
    for cp in cps:
        cp.start()
    for cp in cps:
        cp.wait()


def on_device(hidden, kv_weight, queries, out_grad, live_blocks, doc_start):
    any_ = pl.BlockSpec(memory_space=pl.ANY)
    vmem = pl.BlockSpec(memory_space=pltpu.VMEM)
    vm = pltpu.VMEM
    results = ((ROWS, NH * HD), BF16), ((ROWS, KD), BF16), ((128, KC), F32)
    fused = pl.pallas_call(
        kernel,
        out_shape=tuple(vm(*r) for r in results),
        in_specs=[pl.BlockSpec(memory_space=pltpu.SMEM), vmem, any_, any_, any_, any_],
        out_specs=(vmem, vmem, vmem),
        scratch_shapes=[
            vm((ROWS, KD), BF16), vm((4, 4, 128, ROWS), BF16), vm((4, KD, KC), BF16),
            vm((ROWS, NH * HD), BF16), vm((ROWS, NH * HD), BF16),
            vm((ROWS, KC), F32), vm((ROWS, KC), F32), vm((ROWS, KC), F32), vm((ROWS, KC), F32),
            vm((ROWS, KC), F32), vm((ROWS, KC), F32), vm((ROWS, KC), F32),
            vm((4, ROWS, KC), BF16),
            vm((2, 3, 4, 128, ROWS), BF16),
            vm((2, 3, 2, ROWS, KC), BF16), vm((4, ROWS, KC), F32),
            vm((4, 128, KC), I16), vm((4, 128, KC), I16), vm((4, 128, KC), I16),
            vm((4, 128, KC), I16), vm((4, 128, KC), I16), vm((4, 128, KC), I16),
            vm((3, 4, 8, KC), F32), vm((3, 4, 8, KC), F32),
            vm((4, 128, KC), I16), vm((4, 8, KC), F32), vm((4, 128, KC), I16), vm((4, 8, KC), F32),
            pltpu.SemaphoreType.DMA((N_LOC,)),
            pltpu.SemaphoreType.DMA((N_SEM,)),
            pltpu.SemaphoreType.DMA((N_SEM,)),
        ],
        compiler_params=pltpu.CompilerParams(
            collective_id=0, has_side_effects=True, vmem_limit_bytes=58 * 1024 * 1024
        ),
        name="fused_step",
    )(live_blocks, doc_start.reshape(NB, 128), hidden, kv_weight, queries, out_grad)
    return pl.pallas_call(
        leave,
        out_shape=tuple(jax.ShapeDtypeStruct(*r) for r in results),
        in_specs=[vmem, vmem, vmem],
        out_specs=(any_, any_, any_),
        scratch_shapes=[pltpu.SemaphoreType.DMA((3,))],
        compiler_params=pltpu.CompilerParams(vmem_limit_bytes=1024 * 1024),
        name="leave",
    )(*fused)


def solution(mesh):
    in_specs = (
        P("dp", "tensor"),
        P(None, "tensor"),
        P("dp", "tensor"),
        P("dp", "tensor"),
        P("dp"),
        P("dp"),
    )
    out_specs = (P("dp", "tensor"), P("dp", "tensor"), P("dp", "tensor"))
    return jax.shard_map(
        on_device, mesh=mesh, in_specs=in_specs, out_specs=out_specs, check_vma=False
    )
```
